1024 devices in a mesh: island: 16 (over x, y_hi), fsdp: 8 (over y_lo, core), expert: 8 (over z).
Axes of the slice: x: 8, y: 8 (y_hi: 2, y_lo: 4; y = y_hi * 4 + y_lo), z: 8, core: 2. Of those that a mesh axis runs over, the one named last changes fastest.
Arguments:
- outer_gate: bfloat16 [3072, 8192], P(('fsdp', 'island'), 'expert'), may hold values from -6 to 6
- momentum: float32 [3072, 8192], P(('fsdp', 'island'), 'expert'), may hold values from -4 to 4
- pseudo_grad: bfloat16 [16, 3072, 8192], P('island', 'fsdp', 'expert'), may hold values from -4 to 4
- decay_index: int32 [1], replicated, may hold values from 0 to 32
- inner_weights: bfloat16 [2, 3072, 8192], P(None, 'fsdp', 'expert'), may hold values from -6 to 6
- tokens: bfloat16 [16, 2048, 3072], P('island', 'expert', 'fsdp'), may hold values from -6 to 6
- cotangent: bfloat16 [16, 2048, 3072], P('island', 'expert', 'fsdp'), may hold values from -6 to 6
- routes: int32 [16, 2048, 2], P('island', 'expert'), may hold values from 0 to 7, all different within a row; in each aligned block of 256 rows (0 to 255, 256 to 511, ..., all dimensions but the last counted through in order) at most 64 rows name the same one
- route_weight: float32 [16, 2048, 2], P('island', 'expert'), may hold values from 0.1 to 1
Outputs:
- new_gate: bfloat16 [3072, 8192], P(('fsdp', 'island'), 'expert')
- new_momentum: float32 [3072, 8192], P(('fsdp', 'island'), 'expert')
- token_grad: bfloat16 [16, 2048, 3072], P('island', 'expert', 'fsdp')
The draws below stay inside these ranges and needn't reach their ends.
Inputs may be any that keep to these rules, and one draw needn't show every extreme that they name: `routes`: each token names 2 different experts. Within every aligned block of 256 tokens every expert is named exactly 64 times.
All inputs are finite; a program needn't handle non-finite values.
Results may differ from the reference program's by a relative error of at most 0.013.
Values may be sent and summed in bfloat16 or wider, within the bound.
A program may use at most 32 MiB of HBM per device.

```python
import math
import jax
import jax.numpy as jnp
import numpy as np
from jax import lax

D = 3072
FFW = 8192
EXPERTS = 8
TOP = 2
SCHED = 64
TOK_DEV = 256
ISLANDS = 16
TOKENS = 2048
CAP = 64
SLOTS = 512
N_FSDP = 8


def with_spikes(values, rng, source, target, shards_of, factor):
    def block_of(position):
        return (jnp.arange(values.shape[position]) // (values.shape[position] // shards_of)).reshape((-1,) + (1,) * (values.ndim - 1 - position))

    one_side = jax.random.permutation(rng, shards_of)[block_of(target)]
    other_side = (block_of(target) + shards_of // 2) % shards_of
    return jnp.where((block_of(source) == one_side) | (block_of(source) == other_side), factor * values, values)


def level_of(rng, dims, split, smallest, largest):
    def one(position, blocks):
        steps = jax.random.uniform(jax.random.fold_in(jax.random.fold_in(rng, 6), position), (blocks,), jnp.float32, smallest / len(split), largest / len(split))
        return jnp.repeat(jnp.exp(steps), dims[position] // blocks).reshape((-1,) + (1,) * (len(dims) - position - 1))

    loudness = one(*split[0])
    for cut in split[1:]:
        loudness = loudness * one(*cut)
    return loudness


def deal_out(key, own, number, rows, amount, top, reach, skew):
    order = jax.random.permutation(key, amount)
    heavy_load, ordinary = load_shares(amount, rows * top, reach, skew, True), load_shares(amount, rows * top, reach, skew, False)
    places = jnp.arange(amount)

    def named(sizes, turn):
        used = int((sizes > 0).sum())
        fixed = max(1, used // 4)
        passed = fixed + (places - fixed + turn * (used - fixed)) % max(1, amount - fixed)
        return jnp.zeros((amount,), jnp.int32).at[order[jnp.where(places < fixed, places, passed)]].set(jnp.asarray(sizes, jnp.int32))

    sizes = jnp.where(number % 4 == 0, named(heavy_load, number // 4), named(ordinary, number - number // 4 - 1))
    mixed = jax.random.permutation(jax.random.fold_in(own, 3), amount)
    donor, receiver = mixed[0:amount // 2 * 2:2], mixed[1:amount // 2 * 2:2]
    slack = jnp.minimum(sizes[donor] - 1, reach - sizes[receiver]) // 2
    slack = jnp.where((donor == order[0]) | (receiver == order[0]) | (sizes[receiver] == 0), 0, jnp.maximum(slack, 0))
    passed = jax.random.randint(jax.random.fold_in(own, 4), (amount // 2,), 0, 1 << 20) % (slack + 1)
    sizes = sizes.at[donor].add(-passed).at[receiver].add(passed)
    members = jnp.searchsorted(jnp.cumsum(sizes), jnp.arange(rows * top), side="right").astype(jnp.int32)
    table = members.reshape(top, rows).T
    table = table[jax.random.permutation(jax.random.fold_in(own, 1), rows)]
    turn = jax.random.randint(jax.random.fold_in(own, 2), (rows, 1), 0, top)
    return jnp.take_along_axis(table, (jnp.arange(top)[None, :] + turn) % top, axis=1)


def load_shares(amount, total, reach, lean, full):
    portions = [(1 << 20) // math.isqrt(rank ** lean) + 1 for rank in range(1, amount + 1)]
    largest = reach if full else min(reach, max(-(-total // amount), total * portions[0] // sum(portions)))
    least = 1 if total - largest >= amount - 1 else 0
    counts, rest = [largest] + [least] * (amount - 1), total - largest - least * (amount - 1)
    while rest > 0:
        candidates = [i for i in range(1, amount) if counts[i] < largest] or [i for i in range(1, amount) if counts[i] < reach]
        whole, budget = sum([portions[i] for i in candidates]), rest
        for i in candidates:
            addition = min(reach - counts[i], max(1, budget * portions[i] // whole), rest)
            counts[i] = counts[i] + addition
            rest = rest - addition
    return np.array(counts)


def bell_draw(rng, shape, spread, limit, cuts=(), kind=jnp.bfloat16):
    entries = jax.random.normal(rng, shape, jnp.float32) * spread
    if len(cuts) > 0:
        entries = level_of(rng, shape, cuts, -0.22, 0.18) * entries
    return jnp.clip(entries, min=-limit, max=limit).astype(kind)


def heavy_noise(rng, dims, spread, reach, cuts, heavy, held_as=jnp.bfloat16):
    entries = spread * jax.random.normal(rng, dims, jnp.float32)
    if cuts:
        entries = entries * level_of(rng, dims, cuts, -0.22, 0.18)
    return jnp.clip(with_spikes(entries, jax.random.fold_in(rng, 3), *heavy), -reach, reach).astype(held_as)


def setup_inputs(seed: int = 0) -> dict:
    streams_of = jax.random.split(jax.random.key(seed), 10)
    outer_gate = bell_draw(streams_of[0], (D, FFW), 1.0, 6.0, ((0, 128), (1, 8)))
    momentum = bell_draw(streams_of[1], (D, FFW), 0.5, 4.0, ((0, 128), (1, 8)), jnp.float32)
    pseudo_grad = heavy_noise(streams_of[2], (ISLANDS, D, FFW), 0.5, 4.0, ((0, 16), (1, 8), (2, 8)), (0, 1, 16, 2.0))
    decay_index = jax.random.randint(streams_of[3], (1,), 0, SCHED // 2 + 1).astype(jnp.int32)
    inner_weights = bell_draw(streams_of[4], (2, D, FFW), 1.0, 6.0, ((1, 8), (2, 8)))
    tokens = bell_draw(streams_of[5], (ISLANDS, TOKENS, D), 1.0, 6.0, ((0, 16), (1, 8), (2, 8)))
    cotangent = bell_draw(streams_of[6], (ISLANDS, TOKENS, D), 1.0, 6.0, ((0, 16), (1, 8), (2, 8)))
    routes_keys = jax.random.split(jax.random.fold_in(streams_of[7], 1), ISLANDS * TOKENS // TOK_DEV)
    routes_turns = jax.random.permutation(jax.random.fold_in(streams_of[7], 3), ISLANDS * TOKENS // TOK_DEV)
    routes = jax.vmap(lambda own, number: deal_out(jax.random.fold_in(streams_of[7], 2), own, number, TOK_DEV, EXPERTS, TOP, CAP, 0))(routes_keys, routes_turns).reshape((ISLANDS, TOKENS, TOP))
    route_weight = jnp.clip(0.1 + 0.9 * jax.random.uniform(streams_of[8], (ISLANDS, TOKENS, TOP), jnp.float32) ** level_of(streams_of[8], (ISLANDS, TOKENS, TOP), ((0, 16), (1, 8)), -0.2, 0.2), 0.1, 1.0)
    return {"outer_gate": outer_gate, "momentum": momentum, "pseudo_grad": pseudo_grad, "decay_index": decay_index, "inner_weights": inner_weights, "tokens": tokens, "cotangent": cotangent, "routes": routes, "route_weight": route_weight}


beta_outer = 0.9
rate_outer = 0.7
shrink_rate = 0.2


def swiglu_back(pre_gate, pre_up, back_act):
    sigmoid_gate = jax.nn.sigmoid(pre_gate)
    grad_up = back_act * pre_gate * sigmoid_gate
    grad_gate = back_act * pre_up * sigmoid_gate * (1.0 + pre_gate * (1.0 - sigmoid_gate))
    return grad_gate.astype(jnp.bfloat16), grad_up.astype(jnp.bfloat16)


def block_product(rows, matrix):
    block = D // N_FSDP
    left = rows.astype(jnp.float32).reshape(rows.shape[0], N_FSDP, block)
    right = matrix.astype(jnp.float32).reshape(N_FSDP, block, matrix.shape[1])
    parts = jnp.einsum('sfd,fdh->fsh', left, right)
    return jnp.sum(parts, axis=0)


def island_step(gate_new, up_weight, down_weight, token_rows, cotangent_rows, routes_island, weight_island):
    hit = jnp.sum((routes_island == 0).astype(jnp.int32), axis=1)
    weight_tok = jnp.sum(jnp.where(routes_island == 0, weight_island, 0.0), axis=1).astype(jnp.float32)
    blocks = TOKENS // TOK_DEV
    hit_blocks = hit.reshape(blocks, TOK_DEV)
    rank = jnp.cumsum(hit_blocks, axis=1) - hit_blocks
    column = jnp.arange(blocks, dtype=jnp.int32)[:, None] * CAP + rank
    column = jnp.where(hit_blocks > 0, column, SLOTS).reshape(-1).astype(jnp.int32)
    token_ids = jnp.arange(TOKENS, dtype=jnp.int32)
    table = jnp.full((SLOTS,), TOKENS, dtype=jnp.int32).at[column].set(token_ids, mode="drop")
    slot_weight = jnp.zeros((SLOTS,), dtype=jnp.float32).at[column].set(weight_tok, mode="drop")
    padding = jnp.zeros((1, D), dtype=jnp.bfloat16)
    token_pad = jnp.concatenate([token_rows, padding], axis=0)
    cotangent_pad = jnp.concatenate([cotangent_rows, padding], axis=0)
    routed_tokens = token_pad[table]
    routed_cotangent = (cotangent_pad[table].astype(jnp.float32) * slot_weight[:, None]).astype(jnp.bfloat16)
    in_scale = D ** -0.5
    out_scale = FFW ** -0.5
    pre_gate = in_scale * block_product(routed_tokens, gate_new)
    pre_up = in_scale * block_product(routed_tokens, up_weight)
    back_act = out_scale * block_product(routed_cotangent, down_weight)
    grad_gate, grad_up = swiglu_back(pre_gate, pre_up, back_act)
    slot_grads = in_scale * (jnp.dot(grad_gate, gate_new.T, preferred_element_type=jnp.float32)
                             + jnp.dot(grad_up, up_weight.T, preferred_element_type=jnp.float32))
    slot_grads = slot_grads.astype(jnp.bfloat16)
    summed = jnp.zeros((TOKENS + 1, D), dtype=jnp.float32)
    summed = summed.at[table].add(slot_grads.astype(jnp.float32))
    return summed[:TOKENS].astype(jnp.bfloat16)


def reference(outer_gate, momentum, pseudo_grad, decay_index, inner_weights, tokens, cotangent, routes, route_weight):
    mean_grad = jnp.sum(pseudo_grad.astype(jnp.float32), axis=0) / ISLANDS
    step_value = decay_index.astype(jnp.float32)[0]
    rate_now = rate_outer * 0.5 * (1.0 + jnp.cos(math.pi * step_value / SCHED))
    new_momentum = beta_outer * momentum + mean_grad
    new_gate = ((1.0 - shrink_rate * rate_now) * outer_gate.astype(jnp.float32)
                - rate_now * (mean_grad + beta_outer * new_momentum)).astype(jnp.bfloat16)

    def per_island(packed):
        token_rows, cotangent_rows, routes_island, weight_island = packed
        return island_step(new_gate, inner_weights[0], inner_weights[1], token_rows, cotangent_rows,
                           routes_island, weight_island)

    token_grad = lax.map(per_island, (tokens, cotangent, routes, route_weight))
    return new_gate, new_momentum, token_grad
```

```python
import functools
import math

import jax
import jax.numpy as jnp
from jax import lax
from jax.experimental import pallas as pl
from jax.experimental.pallas import tpu as pltpu
from jax.sharding import PartitionSpec as P

MESH = pl.DeviceIdType.MESH
BF = jnp.bfloat16
F32 = jnp.float32

D = 3072
FFW = 8192
EXPERTS = 8
SCHED = 64
NX, NYL, NZ = 8, 4, 8
ISL = 16
HALF = 512
QUART = 256
SLOTB = 64
ROWS = 48
FWD = (4, 3)
BWD = (3, 4)

beta_outer = 0.9
rate_outer = 0.7
shrink_rate = 0.2


def kernel(pg, mom, og, dec, inner, tok, cot, routes, rw, o_gate, o_mom, o_tok, *scratch):
    (pv, aR, aL, sf, tw_out, tw_in, gown, gst, gbuf, wbuf, xt, xc, placing, uvp, uvsR, uvsL, uvrR, uvrL, uvf, gp, gsR, gsL,
     grR, grL, agL, agR, sgo, sgs, sgr, zs, zrR, zrL, lsem, a_s, a_r, tw_s, tw_r, pc_s, pc_r, x_s, x_r, w_s, w_r, b_s, b_r,
     bs_s, bs_r, uv_s, uv_r, g_s, g_r, ag_s, ag_r, sb_s, sb_r, z_s, z_r) = scratch
    i = lax.axis_index("island")
    f = lax.axis_index("fsdp")
    z = lax.axis_index("expert")
    x, yh = i // 2, i % 2
    yl, c = f // 2, f % 2
    oc = 1 - c

    def dev(dx=0, twin=False, dyl=0, sib=False, dz=0):
        xx = (x + dx + NX) % NX if dx else x
        yy = 1 - yh if twin else yh
        ll = jnp.clip(yl + dyl, 0, NYL - 1) if dyl else yl
        cc = oc if sib else c
        zz = (z + dz + NZ) % NZ if dz else z
        return (xx * 2 + yy, ll * 2 + cc, zz)

    SIB = dev(sib=True)
    TWIN = dev(twin=True)
    TWSIB = dev(twin=True, sib=True)
    XR, XL, ZR, ZL = dev(dx=1), dev(dx=-1), dev(dz=1), dev(dz=-1)
    YR, YL = dev(dyl=1), dev(dyl=-1)

    def rc(src, dst, ss, rs, device):
        return pltpu.make_async_remote_copy(
            src_ref=src, dst_ref=dst, send_sem=ss, recv_sem=rs, device_id=device, device_id_type=MESH)

    sends = []

    def go(src, dst, ss, rs, device):
        cp = rc(src, dst, ss, rs, device)
        cp.start()
        sends.append(cp)

    def got(dst, ss, rs, device):
        rc(dst, dst, ss, rs, device).wait_recv()

    loads = [pltpu.make_async_copy(pg, pv, lsem.at[0])]
    for m in range(2):
        loads.append(pltpu.make_async_copy(
            inner.at[m, :, pl.ds(pl.multiple_of(c * HALF, HALF), HALF)], wbuf.at[m, c], lsem.at[1 + m]))
    for cp in loads:
        cp.start()

    barrier = pltpu.get_barrier_semaphore()
    for device in (XR, XL, ZR, ZL, SIB, TWIN, TWSIB):
        pl.semaphore_signal(barrier, inc=1, device_id=device, device_id_type=MESH)

    @pl.when(yl < NYL - 1)
    def _():
        pl.semaphore_signal(barrier, inc=1, device_id=YR, device_id_type=MESH)

    @pl.when(yl > 0)
    def _():
        pl.semaphore_signal(barrier, inc=1, device_id=YL, device_id_type=MESH)

    pl.semaphore_wait(barrier, 7 + jnp.minimum(yl, 1) + jnp.minimum(NYL - 1 - yl, 1))

    def prow(j):
        return pl.ds(pl.multiple_of(j * ROWS, 16), ROWS)

    def cols(h):
        return pl.ds(h * HALF, HALF)

    def a_step(s):
        for h in range(2):
            for right in (True, False):
                hops = FWD[h] if right else BWD[h]
                if s >= hops:
                    continue
                buf, d0 = (aR, 0) if right else (aL, 1)
                j = (x + hops - s) % NX if right else (x - hops + s + NX) % NX
                q = h * 8 + d0 * 4
                if s == 0:
                    src = pg.at[prow(j), cols(h)]
                else:
                    got(buf.at[h, s - 1], a_s.at[q + s - 1], a_r.at[q + s - 1], XR)
                    total = buf[h, s - 1].astype(F32) + pv[prow(j), cols(h)].astype(F32)
                    buf[h, s - 1] = total.astype(BF)
                    src = buf.at[h, s - 1]
                go(src, buf.at[h, s], a_s.at[q + s], a_r.at[q + s], XR if right else XL)

    a_step(0)

    for m in range(2):
        go(inner.at[m, :, pl.ds(pl.multiple_of(oc * HALF, HALF), HALF)], wbuf.at[m, c], w_s.at[m], w_r.at[m], SIB)

    chosen = routes[...] == 0
    hit = jnp.max(jnp.where(chosen, 1.0, 0.0), axis=0, keepdims=True)
    weight = jnp.sum(jnp.where(chosen, rw[...], 0.0), axis=0, keepdims=True)
    n_tok = hit.shape[1]
    before = (lax.broadcasted_iota(jnp.int32, (n_tok, n_tok), 0)
              < lax.broadcasted_iota(jnp.int32, (n_tok, n_tok), 1))
    rank = jnp.dot(jnp.broadcast_to(hit, (16, n_tok)).astype(BF), jnp.where(before, 1.0, 0.0).astype(BF),
                   preferred_element_type=F32)[0:1, :]
    slot_id = lax.broadcasted_iota(jnp.int32, (SLOTB, n_tok), 0).astype(F32)
    match = jnp.where((slot_id == rank) & (hit > 0.5), 1.0, 0.0)
    slot_weight = jnp.sum(match * weight, axis=1, keepdims=True)
    placing[...] = match.astype(BF)
    xt[z, c] = jnp.dot(placing[...], tok[...], preferred_element_type=F32).astype(BF)
    xc[z, c] = (jnp.dot(placing[...], cot[...], preferred_element_type=F32) * slot_weight).astype(BF)

    XB = (xt, xc)

    def b_sib(m, n, b):
        go(XB[m].at[b, c], XB[m].at[b, c], bs_s.at[m * 8 + n], bs_r.at[m * 8 + n], SIB)

    def b_step(s):
        for m in range(2):
            for right in (True, False):
                hops = FWD[m] if right else BWD[m]
                q = m * 8 + (0 if right else 4)
                if 0 < s <= hops:
                    b = (z - s + NZ) % NZ if right else (z + s) % NZ
                    got(XB[m].at[b, c], b_s.at[q + s - 1], b_r.at[q + s - 1], ZR)
                    b_out = b
                if s < hops:
                    b_out = z if s == 0 else b
                    go(XB[m].at[b_out, c], XB[m].at[b_out, c], b_s.at[q + s], b_r.at[q + s], ZR if right else ZL)
                if 0 < s <= hops:
                    b_sib(m, s if right else FWD[m] + s, b)
            if s == 0:
                b_sib(m, 0, z)

    b_step(0)

    def uv_block(k):
        d = (k + 1) // 2
        return (z - d + NZ) % NZ if (k % 2 == 1) else (z + d) % NZ

    def uv_compute(k):
        b = uv_block(k)
        d = (k + 1) // 2
        for m in range(2):
            if k == 0:
                n = 0
            elif d == 4:
                n = 4 if m == 0 else FWD[1] + 4
            else:
                n = d if k % 2 == 1 else FWD[m] + d
            got(XB[m].at[b, oc], bs_s.at[m * 8 + n], bs_r.at[m * 8 + n], SIB)
        if k == 0:
            for cp in loads[1:]:
                cp.wait()
            for m in range(2):
                got(wbuf.at[m, oc], w_s.at[m], w_r.at[m], SIB)
        for m in range(2):
            uvp[k, m] = (jnp.dot(XB[m][b, 0], wbuf[m, 0], preferred_element_type=F32)
                         + jnp.dot(XB[m][b, 1], wbuf[m, 1], preferred_element_type=F32))

    def uv_right(k, yy):
        part = uvp[k, :, :, QUART:]
        if yy > 0:
            got(uvrR.at[k], uv_s.at[k], uv_r.at[k], YR)
            part = part + uvrR[k].astype(F32)
        if yy < NYL - 1:
            uvsR[k] = part.astype(BF)
            rc(uvsR.at[k], uvrR.at[k], uv_s.at[k], uv_r.at[k], YR).start()
        else:
            uvf[uv_block(k)] = part

    def uv_left(k, yy):
        part = uvp[k, :, :, :QUART]
        if yy < NYL - 1:
            got(uvrL.at[k], uv_s.at[8 + k], uv_r.at[8 + k], YL)
            part = part + uvrL[k].astype(F32)
        if yy > 0:
            uvsL[k] = part.astype(BF)
            rc(uvsL.at[k], uvrL.at[k], uv_s.at[8 + k], uv_r.at[8 + k], YL).start()
        else:
            uvf[uv_block(k)] = part

    def uv_chain(t):
        for yy in range(NYL):
            kr, kl = t - yy, t - (NYL - 1 - yy)

            @pl.when(yl == yy)
            def _():
                for k, side in sorted(((kr, 1), (kl, 0)), reverse=True):
                    if 0 <= k < 8:
                        (uv_right if side else uv_left)(k, yy)

    loads[0].wait()
    a_step(1)
    b_step(1)
    uv_compute(0)
    a_step(2)
    b_step(2)
    uv_compute(1)
    uv_compute(2)
    uv_chain(0)
    a_step(3)
    b_step(3)
    uv_compute(3)
    uv_compute(4)
    uv_chain(1)

    for h in range(2):
        total = pv[prow(x), cols(h)].astype(F32)
        for buf, hops, q in ((aR, FWD[h], h * 8), (aL, BWD[h], h * 8 + 4)):
            got(buf.at[h, hops - 1], a_s.at[q + hops - 1], a_r.at[q + hops - 1], XR)
            total = total + buf[h, hops - 1].astype(F32)
        for half in range(2):
            part = total[half * 24:(half + 1) * 24]
            sf[half, :, h * HALF:(h + 1) * HALF] = part
            tw_out[half, :, h * HALF:(h + 1) * HALF] = part.astype(BF)
    go(tw_out.at[1 - yh], tw_in, tw_s.at[0], tw_r.at[0], TWIN)
    b_step(4)
    uv_compute(5)
    uv_compute(6)
    uv_chain(2)
    uv_compute(7)
    uv_chain(3)

    step_value = jnp.full((8, 128), dec[0], jnp.int32).astype(F32)
    rate = (rate_outer * 0.5 * (1.0 + jnp.cos(math.pi * step_value / SCHED)))[0:1, 0:1]
    got(tw_in, tw_s.at[0], tw_r.at[0], TWIN)
    mean_grad = (sf[yh] + tw_in[...].astype(F32)) * (1.0 / ISL)
    momentum_new = beta_outer * mom[...] + mean_grad
    gate_new = ((1.0 - shrink_rate * rate) * og[...].astype(F32)
                - rate * (mean_grad + beta_outer * momentum_new)).astype(BF)
    gown[0] = gate_new[:, :HALF]
    gown[1] = gate_new[:, HALF:]
    go(gown.at[c], gst.at[yh, c], pc_s.at[0], pc_r.at[0], TWIN)
    go(gown.at[oc], gst.at[yh, c], pc_s.at[1], pc_r.at[1], TWSIB)
    go(gown.at[oc], gst.at[yh, c], pc_s.at[2], pc_r.at[2], SIB)
    gst[yh, c] = gown[c]
    o_gate[...] = gate_new
    o_mom[...] = momentum_new
    uv_chain(4)
    uv_chain(5)
    got(gst.at[1 - yh, c], pc_s.at[0], pc_r.at[0], TWIN)
    got(gst.at[1 - yh, oc], pc_s.at[1], pc_r.at[1], TWSIB)
    got(gst.at[yh, oc], pc_s.at[2], pc_r.at[2], SIB)
    for ff in range(2):
        gbuf[ff, prow(x), :] = jnp.concatenate(
            [gst[0, ff].astype(F32), gst[1, ff].astype(F32)], axis=0).astype(BF)

    def x_step(s):
        for h in range(2):
            for right in (True, False):
                hops = FWD[h] if right else BWD[h]
                q = h * 8 + (0 if right else 4)
                j = (x - s + NX) % NX if right else (x + s) % NX
                here = gbuf.at[h, prow(j), :]
                if 0 < s <= hops:
                    got(here, x_s.at[q + s - 1], x_r.at[q + s - 1], XR)
                if s < hops:
                    go(here, here, x_s.at[q + s], x_r.at[q + s], XR if right else XL)

    for s in range(5):
        x_step(s)
        uv_chain(6 + s)

    in_scale = D ** (-0.5)
    out_scale = FFW ** (-0.5)

    def block_of(k):
        m = 4 - (k + 1) // 2
        sign = 1 - 2 * ((k + 1) % 2)
        return (z + m * sign + NZ) % NZ

    def swiglu(pre, uv):
        pre_gate = in_scale * pre
        pre_up = in_scale * uv[0]
        back = out_scale * uv[1]
        s = jax.nn.sigmoid(pre_gate)
        gu = back * pre_gate * s
        gg = back * pre_up * s * (1.0 + pre_gate * (1.0 - s))
        return gg.astype(BF), gu.astype(BF)

    def go_when(cond, src, dst, ss, rs, device):
        @pl.when(cond)
        def _():
            rc(src, dst, ss, rs, device).start()

    def inside(k):
        return (k >= 0) & (k < 8)

    def g_compute(k):
        b = block_of(k)
        gp[k] = (jnp.dot(xt[b, 0], gbuf[0], preferred_element_type=F32)
                 + jnp.dot(xt[b, 1], gbuf[1], preferred_element_type=F32))

    def g_right(k):
        @pl.when(yl == 0)
        def _():
            gsR[k] = gp[k, :, QUART:].astype(BF)

        @pl.when(yl > 0)
        def _():
            got(grR.at[k], g_s.at[k], g_r.at[k], YR)
            total = gp[k, :, QUART:] + grR[k].astype(F32)

            @pl.when(yl < NYL - 1)
            def _():
                gsR[k] = total.astype(BF)

            @pl.when(yl == NYL - 1)
            def _():
                gg, gu = swiglu(total, uvf[block_of(k)])
                agR[k, 0] = gg
                agR[k, 1] = gu
                rc(agR.at[k], agR.at[k], ag_s.at[k], ag_r.at[k], YL).start()

        go_when(yl < NYL - 1, gsR.at[k], grR.at[k], g_s.at[k], g_r.at[k], YR)

    def g_left(k):
        @pl.when(yl == NYL - 1)
        def _():
            gsL[k] = gp[k, :, :QUART].astype(BF)

        @pl.when(yl < NYL - 1)
        def _():
            got(grL.at[k], g_s.at[8 + k], g_r.at[8 + k], YL)
            total = gp[k, :, :QUART] + grL[k].astype(F32)

            @pl.when(yl > 0)
            def _():
                gsL[k] = total.astype(BF)

            @pl.when(yl == 0)
            def _():
                gg, gu = swiglu(total, uvf[block_of(k)])
                agL[k, 0] = gg
                agL[k, 1] = gu
                rc(agL.at[k], agL.at[k], ag_s.at[8 + k], ag_r.at[8 + k], YR).start()

        go_when(yl > 0, gsL.at[k], grL.at[k], g_s.at[8 + k], g_r.at[8 + k], YL)

    def ag_left_part(k):
        got(agL.at[k], ag_s.at[8 + k], ag_r.at[8 + k], YR)
        go_when(yl < NYL - 1, agL.at[k], agL.at[k], ag_s.at[8 + k], ag_r.at[8 + k], YR)

    def ag_right_part(k):
        got(agR.at[k], ag_s.at[k], ag_r.at[k], YL)
        go_when(yl > 0, agR.at[k], agR.at[k], ag_s.at[k], ag_r.at[k], YL)

    def back(k):
        gg = jnp.concatenate([agL[k, 0], agR[k, 0]], axis=1)
        gu = jnp.concatenate([agL[k, 1], agR[k, 1]], axis=1)
        dims = (((1,), (1,)), ((), ()))

        def part(ff):
            return in_scale * (
                lax.dot_general(gg, gbuf[ff], dims, preferred_element_type=F32)
                + lax.dot_general(gu, wbuf[0, ff], dims, preferred_element_type=F32))

        sgs[k] = part(oc).astype(BF)
        rc(sgs.at[k], sgr.at[k], sb_s.at[k], sb_r.at[k], SIB).start()
        sgo[k] = part(c)

    def z_stage(k):
        got(sgr.at[k], sb_s.at[k], sb_r.at[k], SIB)
        own = sgo[k] + sgr[k].astype(F32)

        @pl.when(k == 0)
        def _():
            zs[k] = own.astype(BF)
            rc(zs.at[k], zrR.at[0], z_s.at[0], z_r.at[0], ZR).start()

        @pl.when((k % 2 == 1) & (k < 7))
        def _():
            s = (k + 1) // 2
            got(zrR.at[s - 1], z_s.at[s - 1], z_r.at[s - 1], ZR)
            zs[k] = (own + zrR[s - 1].astype(F32)).astype(BF)
            rc(zs.at[k], zrR.at[s], z_s.at[s], z_r.at[s], ZR).start()

        @pl.when(k == 2)
        def _():
            zs[k] = own.astype(BF)
            rc(zs.at[k], zrL.at[0], z_s.at[4], z_r.at[4], ZL).start()

        @pl.when((k % 2 == 0) & (k > 2))
        def _():
            s = k // 2 - 1
            got(zrL.at[s - 1], z_s.at[4 + s - 1], z_r.at[4 + s - 1], ZL)
            zs[k] = (own + zrL[s - 1].astype(F32)).astype(BF)
            rc(zs.at[k], zrL.at[s], z_s.at[4 + s], z_r.at[4 + s], ZL).start()

        @pl.when(k == 7)
        def _():
            got(zrR.at[3], z_s.at[3], z_r.at[3], ZR)
            got(zrL.at[2], z_s.at[6], z_r.at[6], ZL)
            slot_grads = (own + zrR[3].astype(F32) + zrL[2].astype(F32)).astype(BF)
            o_tok[...] = lax.dot_general(
                placing[...], slot_grads, (((0,), (0,)), ((), ())), preferred_element_type=F32).astype(BF)

    last = NYL - 1

    def tick(t, carry):
        def stage(k, fn, cond=None):
            ok = inside(k) if cond is None else inside(k) & cond

            @pl.when(ok)
            def _():
                fn(k)

        stage(t, g_compute)
        stage(t - yl, g_right)
        stage(t - (last - yl), g_left)
        stage(t - last - yl, ag_left_part, yl > 0)
        stage(t - last - (last - yl), ag_right_part, yl < last)
        stage(t - 2 * last, back)
        stage(t - 2 * last - 1, z_stage)
        return carry

    lax.fori_loop(0, 8 + 2 * last + 1, tick, None)

    for cp in sends:
        cp.wait_send()

    def drain(k, carry):
        @pl.when(yl < last)
        def _():
            rc(uvsR.at[k], uvrR.at[k], uv_s.at[k], uv_r.at[k], YR).wait_send()
            rc(gsR.at[k], grR.at[k], g_s.at[k], g_r.at[k], YR).wait_send()
            rc(agL.at[k], agL.at[k], ag_s.at[8 + k], ag_r.at[8 + k], YR).wait_send()

        @pl.when(yl > 0)
        def _():
            rc(uvsL.at[k], uvrL.at[k], uv_s.at[8 + k], uv_r.at[8 + k], YL).wait_send()
            rc(gsL.at[k], grL.at[k], g_s.at[8 + k], g_r.at[8 + k], YL).wait_send()
            rc(agR.at[k], agR.at[k], ag_s.at[k], ag_r.at[k], YL).wait_send()

        rc(sgs.at[k], sgr.at[k], sb_s.at[k], sb_r.at[k], SIB).wait_send()

        @pl.when(k < 7)
        def _():
            rc(zs.at[k], zs.at[k], z_s.at[k], z_r.at[k], ZR).wait_send()

        return carry

    lax.fori_loop(0, 8, drain, None)


def local(outer_gate, momentum, pseudo_grad, decay_index, inner_weights, tokens, cotangent, routes, route_weight):
    vmem = pl.BlockSpec(memory_space=pltpu.VMEM)
    hbm = pl.BlockSpec(memory_space=pl.ANY)
    smem = pl.BlockSpec(memory_space=pltpu.SMEM)
    V = pltpu.VMEM
    S = lambda n: pltpu.SemaphoreType.DMA((n,))
    scratch = [
        V((384, 1024), BF), V((2, 4, ROWS, HALF), BF), V((2, 4, ROWS, HALF), BF),
        V((2, 24, 1024), F32), V((2, 24, 1024), BF), V((24, 1024), BF),
        V((2, 24, HALF), BF), V((2, 2, 24, HALF), BF), V((2, 384, HALF), BF),
        V((2, 2, 384, HALF), BF), V((8, 2, SLOTB, 384), BF), V((8, 2, SLOTB, 384), BF),
        V((SLOTB, 256), BF), V((8, 2, SLOTB, HALF), F32),
        V((8, 2, SLOTB, QUART), BF), V((8, 2, SLOTB, QUART), BF), V((8, 2, SLOTB, QUART), BF), V((8, 2, SLOTB, QUART), BF),
        V((8, 2, SLOTB, QUART), F32), V((8, SLOTB, HALF), F32),
        V((8, SLOTB, QUART), BF), V((8, SLOTB, QUART), BF), V((8, SLOTB, QUART), BF), V((8, SLOTB, QUART), BF),
        V((8, 2, SLOTB, QUART), BF), V((8, 2, SLOTB, QUART), BF),
        V((8, SLOTB, 384), F32), V((8, SLOTB, 384), BF), V((8, SLOTB, 384), BF),
        V((8, SLOTB, 384), BF), V((4, SLOTB, 384), BF), V((3, SLOTB, 384), BF),
        S(3), S(16), S(16), S(1), S(1), S(3), S(3), S(16), S(16), S(2), S(2), S(16), S(16), S(16), S(16),
        S(16), S(16), S(16), S(16), S(16), S(16), S(8), S(8), S(7), S(7),
    ]
    new_gate, new_momentum, token_grad = pl.pallas_call(
        kernel,
        out_shape=(
            jax.ShapeDtypeStruct((24, 1024), BF),
            jax.ShapeDtypeStruct((24, 1024), F32),
            jax.ShapeDtypeStruct((256, 384), BF),
        ),
        in_specs=[hbm, vmem, vmem, smem, hbm, vmem, vmem, vmem, vmem],
        out_specs=(vmem, vmem, vmem),
        scratch_shapes=scratch,
        compiler_params=pltpu.CompilerParams(
            collective_id=0, has_side_effects=True, vmem_limit_bytes=48 << 20),
        name="diloco_swiglu",
    )(pseudo_grad[0], momentum, outer_gate, decay_index, inner_weights, tokens[0], cotangent[0], routes[0].T, route_weight[0].T)
    return new_gate, new_momentum, token_grad[None]


def solution(mesh):
    return jax.shard_map(
        local,
        mesh=mesh,
        in_specs=(
            P(("fsdp", "island"), "expert"),
            P(("fsdp", "island"), "expert"),
            P("island", "fsdp", "expert"),
            P(),
            P(None, "fsdp", "expert"),
            P("island", "expert", "fsdp"),
            P("island", "expert", "fsdp"),
            P("island", "expert", None),
            P("island", "expert", None),
        ),
        out_specs=(
            P(("fsdp", "island"), "expert"),
            P(("fsdp", "island"), "expert"),
            P("island", "expert", "fsdp"),
        ),
        check_vma=False,
    )
```

```python
import functools
import math

import jax
import jax.numpy as jnp
from jax import lax
from jax.experimental import pallas as pl
from jax.experimental.pallas import tpu as pltpu
from jax.sharding import PartitionSpec as P

MESH = pl.DeviceIdType.MESH
BF = jnp.bfloat16
F32 = jnp.float32

D = 3072
FFW = 8192
EXPERTS = 8
SCHED = 64
NX, NYL, NZ = 8, 4, 8
ISL = 16
HALF = 512
UVLAG = 2
GLAG = 2
CH = 256
ORDER = (0, 2, 1, 3)
SLOTB = 64
ROWS = 48
FWD = (4, 3)
BWD = (3, 4)

beta_outer = 0.9
rate_outer = 0.7
shrink_rate = 0.2


def kernel(pg, mom_h, og_h, dec, inner, tok_h, cot_h, routes_h, rw_h, o_gate, o_mom, o_tok, *scratch):
    (mom, og, tok, cot, routes, rw, pv, aR, aL, sf, tw_out, tw_in, gown, gst, gbuf, wbuf, xt, xc, placing, uvp, uvsR, uvsL, uvrR, uvrL, gp, gsR, gsL,
     grR, grL, sgo, sgs, sgr, zs, zrR, zrL, lsem, a_s, a_r, tw_s, tw_r, pc_s, pc_r, x_s, x_r, w_s, w_r, b_s, b_r,
     bs_s, bs_r, uv_s, uv_r, g_s, g_r, sb_s, sb_r, z_s, z_r) = scratch
    i = lax.axis_index("island")
    f = lax.axis_index("fsdp")
    z = lax.axis_index("expert")
    x, yh = i // 2, i % 2
    yl, c = f // 2, f % 2
    oc = 1 - c

    def dev(dx=0, twin=False, dyl=0, sib=False, dz=0):
        xx = (x + dx + NX) % NX if dx else x
        yy = 1 - yh if twin else yh
        ll = jnp.clip(yl + dyl, 0, NYL - 1) if dyl else yl
        cc = oc if sib else c
        zz = (z + dz + NZ) % NZ if dz else z
        return (xx * 2 + yy, ll * 2 + cc, zz)

    SIB = dev(sib=True)
    TWIN = dev(twin=True)
    TWSIB = dev(twin=True, sib=True)
    XR, XL, ZR, ZL = dev(dx=1), dev(dx=-1), dev(dz=1), dev(dz=-1)
    YR, YL = dev(dyl=1), dev(dyl=-1)

    def rc(src, dst, ss, rs, device):
        return pltpu.make_async_remote_copy(
            src_ref=src, dst_ref=dst, send_sem=ss, recv_sem=rs, device_id=device, device_id_type=MESH)

    sends = []

    def go(src, dst, ss, rs, device):
        cp = rc(src, dst, ss, rs, device)
        cp.start()
        sends.append(cp)

    def got(dst, ss, rs, device):
        rc(dst, dst, ss, rs, device).wait_recv()

    loads = [pltpu.make_async_copy(pg, pv, lsem.at[0])]
    for m in range(2):
        loads.append(pltpu.make_async_copy(
            inner.at[m, :, pl.ds(pl.multiple_of(c * HALF, HALF), HALF)], wbuf.at[m, c], lsem.at[1 + m]))
    small = [pltpu.make_async_copy(a, b, lsem.at[3 + n]) for n, (a, b) in enumerate(
        ((routes_h, routes), (rw_h, rw), (tok_h, tok), (cot_h, cot), (mom_h, mom), (og_h, og)))]
    for cp in small[:4] + loads + small[4:]:
        cp.start()

    barrier = pltpu.get_barrier_semaphore()
    for device in (XR, XL, ZR, ZL, SIB, TWIN, TWSIB):
        pl.semaphore_signal(barrier, inc=1, device_id=device, device_id_type=MESH)

    @pl.when(yl < NYL - 1)
    def _():
        pl.semaphore_signal(barrier, inc=1, device_id=YR, device_id_type=MESH)

    @pl.when(yl > 0)
    def _():
        pl.semaphore_signal(barrier, inc=1, device_id=YL, device_id_type=MESH)

    pl.semaphore_wait(barrier, 7 + jnp.minimum(yl, 1) + jnp.minimum(NYL - 1 - yl, 1))

    def prow(j):
        return pl.ds(pl.multiple_of(j * ROWS, 16), ROWS)

    def cols(q):
        return pl.ds(q * CH, CH)

    def a_step(s):
        for q in ORDER:
            for right in (True, False):
                hops = FWD[q // 2] if right else BWD[q // 2]
                if s >= hops:
                    continue
                buf, d0 = (aR, 0) if right else (aL, 1)
                j = (x + hops - s) % NX if right else (x - hops + s + NX) % NX
                n = q * 8 + d0 * 4
                if s == 0:
                    src = pg.at[prow(j), cols(q)]
                else:
                    got(buf.at[q, s - 1], a_s.at[n + s - 1], a_r.at[n + s - 1], XR)
                    total = buf[q, s - 1].astype(F32) + pv[prow(j), cols(q)].astype(F32)
                    buf[q, s - 1] = total.astype(BF)
                    src = buf.at[q, s - 1]
                go(src, buf.at[q, s], a_s.at[n + s], a_r.at[n + s], XR if right else XL)

    a_step(0)

    for m in range(2):
        go(inner.at[m, :, pl.ds(pl.multiple_of(oc * HALF, HALF), HALF)], wbuf.at[m, c], w_s.at[m], w_r.at[m], SIB)

    for cp in small[:4]:
        cp.wait()
    chosen = routes[...] == 0
    hit = jnp.max(jnp.where(chosen, 1.0, 0.0), axis=0, keepdims=True)
    weight = jnp.sum(jnp.where(chosen, rw[...], 0.0), axis=0, keepdims=True)
    n_tok = hit.shape[1]
    before = (lax.broadcasted_iota(jnp.int32, (n_tok, n_tok), 0)
              < lax.broadcasted_iota(jnp.int32, (n_tok, n_tok), 1))
    rank = jnp.dot(jnp.broadcast_to(hit, (16, n_tok)).astype(BF), jnp.where(before, 1.0, 0.0).astype(BF),
                   preferred_element_type=F32)[0:1, :]
    slot_id = lax.broadcasted_iota(jnp.int32, (SLOTB, n_tok), 0).astype(F32)
    match = jnp.where((slot_id == rank) & (hit > 0.5), 1.0, 0.0)
    slot_weight = jnp.sum(match * weight, axis=1, keepdims=True)
    placing[...] = match.astype(BF)
    xt[z, c] = jnp.dot(placing[...], tok[...], preferred_element_type=F32).astype(BF)
    xc[z, c] = (jnp.dot(placing[...], cot[...], preferred_element_type=F32) * slot_weight).astype(BF)

    XB = (xt, xc)

    def b_sib(m, n, b):
        go(XB[m].at[b, c], XB[m].at[b, c], bs_s.at[m * 8 + n], bs_r.at[m * 8 + n], SIB)

    def b_step(s):
        for m in range(2):
            for right in (True, False):
                hops = FWD[m] if right else BWD[m]
                q = m * 8 + (0 if right else 4)
                if 0 < s <= hops:
                    b = (z - s + NZ) % NZ if right else (z + s) % NZ
                    got(XB[m].at[b, c], b_s.at[q + s - 1], b_r.at[q + s - 1], ZR)
                    b_out = b
                if s < hops:
                    b_out = z if s == 0 else b
                    go(XB[m].at[b_out, c], XB[m].at[b_out, c], b_s.at[q + s], b_r.at[q + s], ZR if right else ZL)
                if 0 < s <= hops:
                    b_sib(m, s if right else FWD[m] + s, b)
            if s == 0:
                b_sib(m, 0, z)

    b_step(0)

    def uv_block(k):
        d = (k + 1) // 2
        return (z - d + NZ) % NZ if (k % 2 == 1) else (z + d) % NZ

    def uv_compute(k):
        b = uv_block(k)
        d = (k + 1) // 2
        for m in range(2):
            if k == 0:
                n = 0
            elif d == 4:
                n = 4 if m == 0 else FWD[1] + 4
            else:
                n = d if k % 2 == 1 else FWD[m] + d
            got(XB[m].at[b, oc], bs_s.at[m * 8 + n], bs_r.at[m * 8 + n], SIB)
        if k == 0:
            for cp in loads[1:]:
                cp.wait()
            for m in range(2):
                got(wbuf.at[m, oc], w_s.at[m], w_r.at[m], SIB)
        for m in range(2):
            uvp[k, m] = (jnp.dot(XB[m][b, 0], wbuf[m, 0], preferred_element_type=F32)
                         + jnp.dot(XB[m][b, 1], wbuf[m, 1], preferred_element_type=F32))

    last = NYL - 1

    def inside(k):
        return (k >= 0) & (k < 8)

    def chain(k, part, sR, rR, sL, rL, ss, rs, right):
        got_all, out, base, hasin, hasout, to = (
            (rR, sR, 0, yl > 0, yl < last, YR) if right else (rL, sL, 16, yl < last, yl > 0, YL))
        for e in range(2):
            sem = base + 2 * k + e

            @pl.when(inside(k) & hasin)
            def _():
                got(got_all.at[k, e], ss.at[sem], rs.at[sem], to)

            @pl.when(inside(k) & hasout)
            def _():
                out[k, e] = (part[k, e] + got_all[k, e].astype(F32)).astype(BF)
                rc(out.at[k, e], got_all.at[k, e], ss.at[sem], rs.at[sem], to).start()

    def uv_chain(t):
        chain(t - yl * UVLAG, uvp, uvsR, uvrR, uvsL, uvrL, uv_s, uv_r, True)
        chain(t - (last - yl) * UVLAG, uvp, uvsR, uvrR, uvsL, uvrL, uv_s, uv_r, False)

    @pl.when(yl == 0)
    def _():
        uvrR[...] = jnp.zeros_like(uvrR)
        grR[...] = jnp.zeros_like(grR)

    @pl.when(yl == last)
    def _():
        uvrL[...] = jnp.zeros_like(uvrL)
        grL[...] = jnp.zeros_like(grL)

    loads[0].wait()
    a_step(1)
    b_step(1)
    uv_compute(0)
    uv_chain(0)
    a_step(2)
    b_step(2)
    uv_compute(1)
    uv_chain(1)
    uv_compute(2)
    a_step(3)
    b_step(3)
    uv_compute(3)
    uv_chain(2)
    uv_compute(4)

    for q in ORDER:
        total = pv[prow(x), cols(q)].astype(F32)
        for buf, hops, n in ((aR, FWD[q // 2], q * 8), (aL, BWD[q // 2], q * 8 + 4)):
            got(buf.at[q, hops - 1], a_s.at[n + hops - 1], a_r.at[n + hops - 1], XR)
            total = total + buf[q, hops - 1].astype(F32)
        for half in range(2):
            part = total[half * 24:(half + 1) * 24]
            sf[q, half] = part
            tw_out[q, half] = part.astype(BF)
        go(tw_out.at[q, 1 - yh], tw_in.at[q], tw_s.at[q], tw_r.at[q], TWIN)
    b_step(4)
    uv_compute(5)
    uv_chain(3)
    uv_compute(6)
    uv_chain(4)
    uv_compute(7)

    step_value = jnp.full((8, 128), dec[0], jnp.int32).astype(F32)
    rate = (rate_outer * 0.5 * (1.0 + jnp.cos(math.pi * step_value / SCHED)))[0:1, 0:1]
    for cp in small[4:]:
        cp.wait()
    for e in range(2):
        for q in (e, 2 + e):
            where = slice(q * CH, (q + 1) * CH)
            got(tw_in.at[q], tw_s.at[q], tw_r.at[q], TWIN)
            mean_grad = (sf[q, yh] + tw_in[q].astype(F32)) * (1.0 / ISL)
            momentum_new = beta_outer * mom[:, where] + mean_grad
            gate_new = ((1.0 - shrink_rate * rate) * og[:, where].astype(F32)
                        - rate * (mean_grad + beta_outer * momentum_new)).astype(BF)
            gown[q] = gate_new
            o_gate[:, where] = gate_new
            o_mom[:, where] = momentum_new
        go(gown.at[2 * c + e], gst.at[e, yh, c], pc_s.at[3 * e], pc_r.at[3 * e], TWIN)
        go(gown.at[2 * oc + e], gst.at[e, yh, c], pc_s.at[3 * e + 1], pc_r.at[3 * e + 1], TWSIB)
        go(gown.at[2 * oc + e], gst.at[e, yh, c], pc_s.at[3 * e + 2], pc_r.at[3 * e + 2], SIB)
        gst[e, yh, c] = gown[2 * c + e]
    uv_chain(5)

    def x_step(s, e):
        for h in range(2):
            for right in (True, False):
                hops = FWD[h] if right else BWD[h]
                n = (e * 2 + h) * 8 + (0 if right else 4)
                j = (x - s + NX) % NX if right else (x + s) % NX
                here = gbuf.at[e, h, prow(j), :]
                if 0 < s <= hops:
                    got(here, x_s.at[n + s - 1], x_r.at[n + s - 1], XR)
                if s < hops:
                    go(here, here, x_s.at[n + s], x_r.at[n + s], XR if right else XL)

    for e in range(2):
        got(gst.at[e, yh, oc], pc_s.at[3 * e + 2], pc_r.at[3 * e + 2], SIB)
        got(gst.at[e, 1 - yh, c], pc_s.at[3 * e], pc_r.at[3 * e], TWIN)
        got(gst.at[e, 1 - yh, oc], pc_s.at[3 * e + 1], pc_r.at[3 * e + 1], TWSIB)
        for ff in range(2):
            gbuf[e, ff, prow(x), :] = jnp.concatenate(
                [gst[e, 0, ff].astype(F32), gst[e, 1, ff].astype(F32)], axis=0).astype(BF)
        x_step(0, e)
    uv_chain(6)
    for s in range(1, 5):
        for e in range(2):
            x_step(s, e)
        if s < 4:
            uv_chain(6 + s)

    in_scale = D ** (-0.5)
    out_scale = FFW ** (-0.5)

    def block_of(k):
        m = 4 - (k + 1) // 2
        sign = 1 - 2 * ((k + 1) % 2)
        return (z + m * sign + NZ) % NZ

    def swiglu(pre, uv):
        pre_gate = in_scale * pre
        pre_up = in_scale * uv[0]
        back = out_scale * uv[1]
        s = jax.nn.sigmoid(pre_gate)
        gu = back * pre_gate * s
        gg = back * pre_up * s * (1.0 + pre_gate * (1.0 - s))
        return gg.astype(BF), gu.astype(BF)

    def g_compute(k):
        b = block_of(k)
        for e in range(2):
            gp[k, e] = (jnp.dot(xt[b, 0], gbuf[e, 0], preferred_element_type=F32)
                        + jnp.dot(xt[b, 1], gbuf[e, 1], preferred_element_type=F32))

    def back(k):
        u = 7 - k
        dims = (((1,), (1,)), ((), ()))
        grads = []
        for e in range(2):
            where = slice(e * CH, (e + 1) * CH)
            pre = gp[k, e] + grR[k, e].astype(F32) + grL[k, e].astype(F32)
            uv = [uvp[u, m, :, where] + uvrR[u, m, :, where].astype(F32) + uvrL[u, m, :, where].astype(F32) for m in range(2)]
            grads.append(swiglu(pre, uv))

        def part(ff):
            total = 0.0
            for e, (gg, gu) in enumerate(grads):
                total = total + lax.dot_general(gg, gbuf[e, ff], dims, preferred_element_type=F32)
                total = total + lax.dot_general(
                    gu, wbuf[0, ff, :, e * CH:(e + 1) * CH], dims, preferred_element_type=F32)
            return in_scale * total

        sgs[k] = part(oc).astype(BF)
        rc(sgs.at[k], sgr.at[k], sb_s.at[k], sb_r.at[k], SIB).start()
        sgo[k] = part(c)

    def z_stage(k):
        got(sgr.at[k], sb_s.at[k], sb_r.at[k], SIB)
        own = sgo[k] + sgr[k].astype(F32)

        @pl.when(k == 0)
        def _():
            zs[k] = own.astype(BF)
            rc(zs.at[k], zrR.at[0], z_s.at[0], z_r.at[0], ZR).start()

        @pl.when((k % 2 == 1) & (k < 7))
        def _():
            s = (k + 1) // 2
            got(zrR.at[s - 1], z_s.at[s - 1], z_r.at[s - 1], ZR)
            zs[k] = (own + zrR[s - 1].astype(F32)).astype(BF)
            rc(zs.at[k], zrR.at[s], z_s.at[s], z_r.at[s], ZR).start()

        @pl.when(k == 2)
        def _():
            zs[k] = own.astype(BF)
            rc(zs.at[k], zrL.at[0], z_s.at[4], z_r.at[4], ZL).start()

        @pl.when((k % 2 == 0) & (k > 2))
        def _():
            s = k // 2 - 1
            got(zrL.at[s - 1], z_s.at[4 + s - 1], z_r.at[4 + s - 1], ZL)
            zs[k] = (own + zrL[s - 1].astype(F32)).astype(BF)
            rc(zs.at[k], zrL.at[s], z_s.at[4 + s], z_r.at[4 + s], ZL).start()

        @pl.when(k == 7)
        def _():
            got(zrR.at[3], z_s.at[3], z_r.at[3], ZR)
            got(zrL.at[2], z_s.at[6], z_r.at[6], ZL)
            slot_grads = (own + zrR[3].astype(F32) + zrL[2].astype(F32)).astype(BF)
            o_tok[...] = lax.dot_general(
                placing[...], slot_grads, (((0,), (0,)), ((), ())), preferred_element_type=F32).astype(BF)

    def tick(t, carry):
        def stage(k, fn):
            @pl.when(inside(k))
            def _():
                fn(k)

        chain(t - yl * GLAG, gp, gsR, grR, gsL, grL, g_s, g_r, True)
        chain(t - (last - yl) * GLAG, gp, gsR, grR, gsL, grL, g_s, g_r, False)
        uv_chain(t + 10)
        stage(t + 1, g_compute)
        stage(t - last * GLAG, back)
        stage(t - last * GLAG - 1, z_stage)
        return carry

    g_compute(0)
    lax.fori_loop(0, 8 + last * GLAG + 1, tick, None)

    for cp in sends:
        cp.wait_send()

    def drain(k, carry):
        for e in range(2):
            n = 2 * k + e

            @pl.when(yl < last)
            def _():
                rc(uvsR.at[k, e], uvrR.at[k, e], uv_s.at[n], uv_r.at[n], YR).wait_send()
                rc(gsR.at[k, e], grR.at[k, e], g_s.at[n], g_r.at[n], YR).wait_send()

            @pl.when(yl > 0)
            def _():
                rc(uvsL.at[k, e], uvrL.at[k, e], uv_s.at[16 + n], uv_r.at[16 + n], YL).wait_send()
                rc(gsL.at[k, e], grL.at[k, e], g_s.at[16 + n], g_r.at[16 + n], YL).wait_send()

        rc(sgs.at[k], sgr.at[k], sb_s.at[k], sb_r.at[k], SIB).wait_send()

        @pl.when(k < 7)
        def _():
            rc(zs.at[k], zs.at[k], z_s.at[k], z_r.at[k], ZR).wait_send()

        return carry

    lax.fori_loop(0, 8, drain, None)


def local(outer_gate, momentum, pseudo_grad, decay_index, inner_weights, tokens, cotangent, routes, route_weight):
    vmem = pl.BlockSpec(memory_space=pltpu.VMEM)
    hbm = pl.BlockSpec(memory_space=pltpu.HBM)
    smem = pl.BlockSpec(memory_space=pltpu.SMEM)
    V = pltpu.VMEM
    S = lambda n: pltpu.SemaphoreType.DMA((n,))
    scratch = [
        V((24, 1024), F32), V((24, 1024), BF), V((256, 384), BF), V((256, 384), BF), V((2, 256), jnp.int32), V((2, 256), F32),
        V((384, 1024), BF), V((4, 4, ROWS, CH), BF), V((4, 4, ROWS, CH), BF),
        V((4, 2, 24, CH), F32), V((4, 2, 24, CH), BF), V((4, 24, CH), BF),
        V((4, 24, CH), BF), V((2, 2, 2, 24, CH), BF), V((2, 2, 384, CH), BF),
        V((2, 2, 384, HALF), BF), V((8, 2, SLOTB, 384), BF), V((8, 2, SLOTB, 384), BF),
        V((SLOTB, 256), BF), V((8, 2, SLOTB, HALF), F32),
        V((8, 2, SLOTB, HALF), BF), V((8, 2, SLOTB, HALF), BF), V((8, 2, SLOTB, HALF), BF), V((8, 2, SLOTB, HALF), BF),
        V((8, 2, SLOTB, CH), F32),
        V((8, 2, SLOTB, CH), BF), V((8, 2, SLOTB, CH), BF), V((8, 2, SLOTB, CH), BF), V((8, 2, SLOTB, CH), BF),
        V((8, SLOTB, 384), F32), V((8, SLOTB, 384), BF), V((8, SLOTB, 384), BF),
        V((8, SLOTB, 384), BF), V((4, SLOTB, 384), BF), V((3, SLOTB, 384), BF),
        S(9), S(32), S(32), S(4), S(4), S(6), S(6), S(32), S(32), S(2), S(2), S(16), S(16), S(16), S(16),
        S(32), S(32), S(32), S(32), S(8), S(8), S(7), S(7),
    ]
    new_gate, new_momentum, token_grad = pl.pallas_call(
        kernel,
        out_shape=(
            jax.ShapeDtypeStruct((24, 1024), BF),
            jax.ShapeDtypeStruct((24, 1024), F32),
            jax.ShapeDtypeStruct((256, 384), BF),
        ),
        in_specs=[hbm, hbm, hbm, smem, hbm, hbm, hbm, hbm, hbm],
        out_specs=(vmem, vmem, vmem),
        scratch_shapes=scratch,
        compiler_params=pltpu.CompilerParams(
            collective_id=0, has_side_effects=True, vmem_limit_bytes=67_000_000),
        name="diloco_swiglu",
    )(pseudo_grad[0], momentum, outer_gate, decay_index, inner_weights, tokens[0], cotangent[0], routes[0].T, route_weight[0].T)
    return new_gate, new_momentum, token_grad[None]


def solution(mesh):
    return jax.shard_map(
        local,
        mesh=mesh,
        in_specs=(
            P(("fsdp", "island"), "expert"),
            P(("fsdp", "island"), "expert"),
            P("island", "fsdp", "expert"),
            P(),
            P(None, "fsdp", "expert"),
            P("island", "expert", "fsdp"),
            P("island", "expert", "fsdp"),
            P("island", "expert", None),
            P("island", "expert", None),
        ),
        out_specs=(
            P(("fsdp", "island"), "expert"),
            P(("fsdp", "island"), "expert"),
            P("island", "expert", "fsdp"),
        ),
        check_vma=False,
    )
```

```python
import functools
import math

import jax
import jax.numpy as jnp
from jax import lax
from jax.experimental import pallas as pl
from jax.experimental.pallas import tpu as pltpu
from jax.sharding import PartitionSpec as P

MESH = pl.DeviceIdType.MESH
BF = jnp.bfloat16
F32 = jnp.float32

D = 3072
FFW = 8192
EXPERTS = 8
SCHED = 64
NX, NYL, NZ = 8, 4, 8
ISL = 16
HALF = 512
UVLAG = 2
GLAG = 2
CH = 256
SLOTB = 64
ROWS = 48
FWD = (4, 3)
BWD = (3, 4)

beta_outer = 0.9
rate_outer = 0.7
shrink_rate = 0.2


def kernel(pg, mom_h, og_h, dec, inner, tok_h, cot_h, routes_h, rw_h, o_gate, o_mom, o_tok, *scratch):
    (momb, ogb, tok, cot, routes, rw, pv, aR, aL, sf, tw_out, tw_in, mall, gall, mfin, gfin, gbuf, wbuf, xt, xc, placing, uvp, uvsR, uvsL, uvrR, uvrL, gp, gsR, gsL,
     grR, grL, sgo, sgs, sgr, zs, zrR, zrL, lsem, a_s, a_r, tw_s, tw_r, pp_s, pp_r, me_s, me_r, of_s, of_r, x_s, x_r, w_s, w_r, b_s, b_r,
     bs_s, bs_r, uv_s, uv_r, g_s, g_r, sb_s, sb_r, z_s, z_r) = scratch
    i = lax.axis_index("island")
    f = lax.axis_index("fsdp")
    z = lax.axis_index("expert")
    x, yh = i // 2, i % 2
    yl, c = f // 2, f % 2
    oc = 1 - c

    def dev(dx=0, twin=False, dyl=0, sib=False, dz=0):
        xx = (x + dx + NX) % NX if dx else x
        yy = 1 - yh if twin else yh
        ll = jnp.clip(yl + dyl, 0, NYL - 1) if dyl else yl
        cc = oc if sib else c
        zz = (z + dz + NZ) % NZ if dz else z
        return (xx * 2 + yy, ll * 2 + cc, zz)

    SIB = dev(sib=True)
    TWIN = dev(twin=True)
    TWSIB = dev(twin=True, sib=True)
    XR, XL, ZR, ZL = dev(dx=1), dev(dx=-1), dev(dz=1), dev(dz=-1)
    XRS, XLS = dev(dx=1, sib=True), dev(dx=-1, sib=True)
    YR, YL = dev(dyl=1), dev(dyl=-1)

    def rc(src, dst, ss, rs, device):
        return pltpu.make_async_remote_copy(
            src_ref=src, dst_ref=dst, send_sem=ss, recv_sem=rs, device_id=device, device_id_type=MESH)

    sends = []

    def go(src, dst, ss, rs, device):
        cp = rc(src, dst, ss, rs, device)
        cp.start()
        sends.append(cp)

    def got(dst, ss, rs, device):
        rc(dst, dst, ss, rs, device).wait_recv()

    def half_cols(half, first=0, size=HALF):
        return pl.ds(pl.multiple_of(half * HALF + first, CH), size)

    loads = [pltpu.make_async_copy(pg.at[:, half_cols(c)], pv.at[c], lsem.at[0])]
    for m in range(2):
        loads.append(pltpu.make_async_copy(
            inner.at[m, :, pl.ds(pl.multiple_of(c * HALF, HALF), HALF)], wbuf.at[m, c], lsem.at[1 + m]))
    small = [pltpu.make_async_copy(a, b, lsem.at[3 + n]) for n, (a, b) in enumerate(
        ((routes_h, routes), (rw_h, rw), (tok_h, tok), (cot_h, cot), (mom_h.at[:, half_cols(c)], momb.at[c, yh]), (og_h.at[:, half_cols(c)], ogb.at[c, yh])))]
    for cp in small[:4] + loads + small[4:]:
        cp.start()

    barrier = pltpu.get_barrier_semaphore()
    for device in (XR, XL, XRS, XLS, ZR, ZL, SIB, TWIN, TWSIB):
        pl.semaphore_signal(barrier, inc=1, device_id=device, device_id_type=MESH)

    @pl.when(yl < NYL - 1)
    def _():
        pl.semaphore_signal(barrier, inc=1, device_id=YR, device_id_type=MESH)

    @pl.when(yl > 0)
    def _():
        pl.semaphore_signal(barrier, inc=1, device_id=YL, device_id_type=MESH)

    pl.semaphore_wait(barrier, 9 + jnp.minimum(yl, 1) + jnp.minimum(NYL - 1 - yl, 1))

    def prow(j):
        return pl.ds(pl.multiple_of(j * ROWS, 16), ROWS)

    def a_step(s):
        for e in range(2):
            for ff in range(2):
                for right in (True, False):
                    hops = FWD[e] if right else BWD[e]
                    if s >= hops:
                        continue
                    buf, d0 = (aR, 0) if right else (aL, 4)
                    j = (x + hops - s) % NX if right else (x - hops + s + NX) % NX
                    if s == 0:
                        half = oc if ff else c
                        to = (XRS if right else XLS) if ff else (XR if right else XL)
                        go(pg.at[prow(j), half_cols(half, e * CH, CH)], buf.at[2 * c + e, 0],
                           a_s.at[(2 * half + e) * 8 + d0], a_r.at[(2 * c + e) * 8 + d0], to)
                    else:
                        q = 2 * ff + e
                        n = q * 8 + d0 + s
                        got(buf.at[q, s - 1], a_s.at[n - 1], a_r.at[n - 1], XR)
                        total = buf[q, s - 1].astype(F32) + pv[ff, prow(j), e * CH:(e + 1) * CH].astype(F32)
                        buf[q, s - 1] = total.astype(BF)
                        go(buf.at[q, s - 1], buf.at[q, s], a_s.at[n], a_r.at[n], XR if right else XL)

    a_step(0)
    go(pg.at[:, half_cols(oc)], pv.at[c], pp_s.at[0], pp_r.at[0], SIB)

    for m in range(2):
        go(inner.at[m, :, pl.ds(pl.multiple_of(oc * HALF, HALF), HALF)], wbuf.at[m, c], w_s.at[m], w_r.at[m], SIB)

    for n, (half, to) in enumerate(((c, TWIN), (oc, SIB), (oc, TWSIB))):
        go(mom_h.at[:, half_cols(half)], momb.at[c, yh], me_s.at[2 * n], me_r.at[2 * n], to)
        go(og_h.at[:, half_cols(half)], ogb.at[c, yh], me_s.at[2 * n + 1], me_r.at[2 * n + 1], to)

    for cp in small[:4]:
        cp.wait()
    chosen = routes[...] == 0
    hit = jnp.max(jnp.where(chosen, 1.0, 0.0), axis=0, keepdims=True)
    weight = jnp.sum(jnp.where(chosen, rw[...], 0.0), axis=0, keepdims=True)
    n_tok = hit.shape[1]
    before = (lax.broadcasted_iota(jnp.int32, (n_tok, n_tok), 0)
              < lax.broadcasted_iota(jnp.int32, (n_tok, n_tok), 1))
    rank = jnp.dot(jnp.broadcast_to(hit, (16, n_tok)).astype(BF), jnp.where(before, 1.0, 0.0).astype(BF),
                   preferred_element_type=F32)[0:1, :]
    slot_id = lax.broadcasted_iota(jnp.int32, (SLOTB, n_tok), 0).astype(F32)
    match = jnp.where((slot_id == rank) & (hit > 0.5), 1.0, 0.0)
    slot_weight = jnp.sum(match * weight, axis=1, keepdims=True)
    placing[...] = match.astype(BF)
    xt[z, c] = jnp.dot(placing[...], tok[...], preferred_element_type=F32).astype(BF)
    xc[z, c] = (jnp.dot(placing[...], cot[...], preferred_element_type=F32) * slot_weight).astype(BF)

    XB = (xt, xc)

    def b_sib(m, n, b):
        go(XB[m].at[b, c], XB[m].at[b, c], bs_s.at[m * 8 + n], bs_r.at[m * 8 + n], SIB)

    def b_step(s):
        for m in range(2):
            for right in (True, False):
                hops = FWD[m] if right else BWD[m]
                q = m * 8 + (0 if right else 4)
                if 0 < s <= hops:
                    b = (z - s + NZ) % NZ if right else (z + s) % NZ
                    got(XB[m].at[b, c], b_s.at[q + s - 1], b_r.at[q + s - 1], ZR)
                    b_out = b
                if s < hops:
                    b_out = z if s == 0 else b
                    go(XB[m].at[b_out, c], XB[m].at[b_out, c], b_s.at[q + s], b_r.at[q + s], ZR if right else ZL)
                if 0 < s <= hops:
                    b_sib(m, s if right else FWD[m] + s, b)
            if s == 0:
                b_sib(m, 0, z)

    b_step(0)

    def uv_block(k):
        d = (k + 1) // 2
        return (z - d + NZ) % NZ if (k % 2 == 1) else (z + d) % NZ

    def uv_compute(k):
        b = uv_block(k)
        d = (k + 1) // 2
        for m in range(2):
            if k == 0:
                n = 0
            elif d == 4:
                n = 4 if m == 0 else FWD[1] + 4
            else:
                n = d if k % 2 == 1 else FWD[m] + d
            got(XB[m].at[b, oc], bs_s.at[m * 8 + n], bs_r.at[m * 8 + n], SIB)
        if k == 0:
            for cp in loads[1:]:
                cp.wait()
            for m in range(2):
                got(wbuf.at[m, oc], w_s.at[m], w_r.at[m], SIB)
        for m in range(2):
            uvp[k, m] = (jnp.dot(XB[m][b, 0], wbuf[m, 0], preferred_element_type=F32)
                         + jnp.dot(XB[m][b, 1], wbuf[m, 1], preferred_element_type=F32))

    last = NYL - 1

    def inside(k):
        return (k >= 0) & (k < 8)

    def chain(k, part, sR, rR, sL, rL, ss, rs, right):
        got_all, out, base, hasin, hasout, to = (
            (rR, sR, 0, yl > 0, yl < last, YR) if right else (rL, sL, 16, yl < last, yl > 0, YL))
        for e in range(2):
            sem = base + 2 * k + e

            @pl.when(inside(k) & hasin)
            def _():
                got(got_all.at[k, e], ss.at[sem], rs.at[sem], to)

            @pl.when(inside(k) & hasout)
            def _():
                out[k, e] = (part[k, e] + got_all[k, e].astype(F32)).astype(BF)
                rc(out.at[k, e], got_all.at[k, e], ss.at[sem], rs.at[sem], to).start()

    def uv_chain(t):
        chain(t - yl * UVLAG, uvp, uvsR, uvrR, uvsL, uvrL, uv_s, uv_r, True)
        chain(t - (last - yl) * UVLAG, uvp, uvsR, uvrR, uvsL, uvrL, uv_s, uv_r, False)

    @pl.when(yl == 0)
    def _():
        uvrR[...] = jnp.zeros_like(uvrR)
        grR[...] = jnp.zeros_like(grR)

    @pl.when(yl == last)
    def _():
        uvrL[...] = jnp.zeros_like(uvrL)
        grL[...] = jnp.zeros_like(grL)

    loads[0].wait()
    got(pv.at[oc], pp_s.at[0], pp_r.at[0], SIB)
    a_step(1)
    b_step(1)
    uv_compute(0)
    uv_chain(0)
    a_step(2)
    uv_compute(1)
    b_step(2)
    uv_chain(1)
    a_step(3)
    uv_compute(2)
    b_step(3)
    uv_compute(3)
    uv_chain(2)

    for e in range(2):
        for ff in range(2):
            q = 2 * ff + e
            total = pv[ff, prow(x), e * CH:(e + 1) * CH].astype(F32)
            for buf, hops, n in ((aR, FWD[e], q * 8), (aL, BWD[e], q * 8 + 4)):
                got(buf.at[q, hops - 1], a_s.at[n + hops - 1], a_r.at[n + hops - 1], XR)
                total = total + buf[q, hops - 1].astype(F32)
            sf[q] = total
            tw_out[q] = total.astype(BF)
            go(tw_out.at[q], tw_in.at[q], tw_s.at[q], tw_r.at[q], TWIN)
    uv_compute(4)
    uv_compute(5)
    b_step(4)
    uv_chain(3)
    uv_compute(6)
    uv_compute(7)

    step_value = jnp.full((8, 128), dec[0], jnp.int32).astype(F32)
    rate = (rate_outer * 0.5 * (1.0 + jnp.cos(math.pi * step_value / SCHED)))[0:1, 0:1]
    for cp in small[4:]:
        cp.wait()
    for n, (ff, hh, to) in enumerate(((c, 1 - yh, TWIN), (oc, yh, SIB), (oc, 1 - yh, TWSIB))):
        got(momb.at[ff, hh], me_s.at[2 * n], me_r.at[2 * n], to)
        got(ogb.at[ff, hh], me_s.at[2 * n + 1], me_r.at[2 * n + 1], to)

    def outer_step(e):
        where = slice(e * CH, (e + 1) * CH)
        for ff in range(2):
            q = 2 * ff + e
            got(tw_in.at[q], tw_s.at[q], tw_r.at[q], TWIN)
            mean_grad = (sf[q] + tw_in[q].astype(F32)) * (1.0 / ISL)
            old = jnp.concatenate([momb[ff, 0, :, where], momb[ff, 1, :, where]], axis=0)
            outer = jnp.concatenate([ogb[ff, 0, :, where].astype(F32), ogb[ff, 1, :, where].astype(F32)], axis=0)
            momentum_new = beta_outer * old + mean_grad
            gate_new = (1.0 - shrink_rate * rate) * outer - rate * (mean_grad + beta_outer * momentum_new)
            gbuf[e, ff, prow(x), :] = gate_new.astype(BF)
            for hh in range(2):
                mall[q, hh] = momentum_new[hh * 24:(hh + 1) * 24]
                gall[q, hh] = gate_new[hh * 24:(hh + 1) * 24].astype(BF)

    def hand_out(e):
        mfin[c, e] = mall[2 * c + e, yh]
        gfin[c, e] = gall[2 * c + e, yh]
        go(mall.at[2 * oc + e, yh], mfin.at[c, e], of_s.at[2 * e], of_r.at[2 * e], SIB)
        go(gall.at[2 * oc + e, yh], gfin.at[c, e], of_s.at[2 * e + 1], of_r.at[2 * e + 1], SIB)

    def x_step(s, e):
        for h in range(2):
            for right in (True, False):
                hops = FWD[h] if right else BWD[h]
                n = (e * 2 + h) * 8 + (0 if right else 4)
                j = (x - s + NX) % NX if right else (x + s) % NX
                here = gbuf.at[e, h, prow(j), :]
                if 0 < s <= hops:
                    got(here, x_s.at[n + s - 1], x_r.at[n + s - 1], XR)
                if s < hops:
                    go(here, here, x_s.at[n + s], x_r.at[n + s], XR if right else XL)

    for e in range(2):
        outer_step(e)
        x_step(0, e)
    uv_chain(4)
    for e in range(2):
        hand_out(e)
    uv_chain(5)
    for s in range(1, 5):
        for e in range(2):
            x_step(s, e)
        if s < 4:
            uv_chain(5 + s)

    in_scale = D ** (-0.5)
    out_scale = FFW ** (-0.5)

    def block_of(k):
        m = 4 - (k + 1) // 2
        sign = 1 - 2 * ((k + 1) % 2)
        return (z + m * sign + NZ) % NZ

    def swiglu(pre, uv):
        pre_gate = in_scale * pre
        pre_up = in_scale * uv[0]
        back = out_scale * uv[1]
        s = jax.nn.sigmoid(pre_gate)
        gu = back * pre_gate * s
        gg = back * pre_up * s * (1.0 + pre_gate * (1.0 - s))
        return gg.astype(BF), gu.astype(BF)

    def g_compute(k):
        b = block_of(k)
        for e in range(2):
            gp[k, e] = (jnp.dot(xt[b, 0], gbuf[e, 0], preferred_element_type=F32)
                        + jnp.dot(xt[b, 1], gbuf[e, 1], preferred_element_type=F32))

    def back(k):
        u = 7 - k
        dims = (((1,), (1,)), ((), ()))
        grads = []
        for e in range(2):
            where = slice(e * CH, (e + 1) * CH)
            pre = gp[k, e] + grR[k, e].astype(F32) + grL[k, e].astype(F32)
            uv = [uvp[u, m, :, where] + uvrR[u, m, :, where].astype(F32) + uvrL[u, m, :, where].astype(F32) for m in range(2)]
            grads.append(swiglu(pre, uv))

        def part(ff):
            total = 0.0
            for e, (gg, gu) in enumerate(grads):
                total = total + lax.dot_general(gg, gbuf[e, ff], dims, preferred_element_type=F32)
                total = total + lax.dot_general(
                    gu, wbuf[0, ff, :, e * CH:(e + 1) * CH], dims, preferred_element_type=F32)
            return in_scale * total

        sgs[k] = part(oc).astype(BF)
        rc(sgs.at[k], sgr.at[k], sb_s.at[k], sb_r.at[k], SIB).start()
        sgo[k] = part(c)

    def z_stage(k):
        got(sgr.at[k], sb_s.at[k], sb_r.at[k], SIB)
        own = sgo[k] + sgr[k].astype(F32)

        @pl.when(k == 0)
        def _():
            zs[k] = own.astype(BF)
            rc(zs.at[k], zrR.at[0], z_s.at[0], z_r.at[0], ZR).start()

        @pl.when((k % 2 == 1) & (k < 7))
        def _():
            s = (k + 1) // 2
            got(zrR.at[s - 1], z_s.at[s - 1], z_r.at[s - 1], ZR)
            zs[k] = (own + zrR[s - 1].astype(F32)).astype(BF)
            rc(zs.at[k], zrR.at[s], z_s.at[s], z_r.at[s], ZR).start()

        @pl.when(k == 2)
        def _():
            zs[k] = own.astype(BF)
            rc(zs.at[k], zrL.at[0], z_s.at[4], z_r.at[4], ZL).start()

        @pl.when((k % 2 == 0) & (k > 2))
        def _():
            s = k // 2 - 1
            got(zrL.at[s - 1], z_s.at[4 + s - 1], z_r.at[4 + s - 1], ZL)
            zs[k] = (own + zrL[s - 1].astype(F32)).astype(BF)
            rc(zs.at[k], zrL.at[s], z_s.at[4 + s], z_r.at[4 + s], ZL).start()

        @pl.when(k == 7)
        def _():
            got(zrR.at[3], z_s.at[3], z_r.at[3], ZR)
            got(zrL.at[2], z_s.at[6], z_r.at[6], ZL)
            slot_grads = (own + zrR[3].astype(F32) + zrL[2].astype(F32)).astype(BF)
            o_tok[...] = lax.dot_general(
                placing[...], slot_grads, (((0,), (0,)), ((), ())), preferred_element_type=F32).astype(BF)

    def tick(t, carry):
        def stage(k, fn):
            @pl.when(inside(k))
            def _():
                fn(k)

        chain(t - yl * GLAG, gp, gsR, grR, gsL, grL, g_s, g_r, True)
        chain(t - (last - yl) * GLAG, gp, gsR, grR, gsL, grL, g_s, g_r, False)
        uv_chain(t + 9)
        stage(t - last * GLAG, back)
        stage(t - last * GLAG - 1, z_stage)
        stage(t + 1, g_compute)
        return carry

    g_compute(0)
    lax.fori_loop(0, 8 + last * GLAG + 1, tick, None)

    for e in range(2):
        got(mfin.at[oc, e], of_s.at[2 * e], of_r.at[2 * e], SIB)
        got(gfin.at[oc, e], of_s.at[2 * e + 1], of_r.at[2 * e + 1], SIB)
        for half in range(2):
            where = slice(half * HALF + e * CH, half * HALF + (e + 1) * CH)
            o_mom[:, where] = mfin[half, e]
            o_gate[:, where] = gfin[half, e]

    for cp in sends:
        cp.wait_send()

    def drain(k, carry):
        for e in range(2):
            n = 2 * k + e

            @pl.when(yl < last)
            def _():
                rc(uvsR.at[k, e], uvrR.at[k, e], uv_s.at[n], uv_r.at[n], YR).wait_send()
                rc(gsR.at[k, e], grR.at[k, e], g_s.at[n], g_r.at[n], YR).wait_send()

            @pl.when(yl > 0)
            def _():
                rc(uvsL.at[k, e], uvrL.at[k, e], uv_s.at[16 + n], uv_r.at[16 + n], YL).wait_send()
                rc(gsL.at[k, e], grL.at[k, e], g_s.at[16 + n], g_r.at[16 + n], YL).wait_send()

        rc(sgs.at[k], sgr.at[k], sb_s.at[k], sb_r.at[k], SIB).wait_send()

        @pl.when(k < 7)
        def _():
            rc(zs.at[k], zs.at[k], z_s.at[k], z_r.at[k], ZR).wait_send()

        return carry

    lax.fori_loop(0, 8, drain, None)


def local(outer_gate, momentum, pseudo_grad, decay_index, inner_weights, tokens, cotangent, routes, route_weight):
    vmem = pl.BlockSpec(memory_space=pltpu.VMEM)
    hbm = pl.BlockSpec(memory_space=pltpu.HBM)
    smem = pl.BlockSpec(memory_space=pltpu.SMEM)
    V = pltpu.VMEM
    S = lambda n: pltpu.SemaphoreType.DMA((n,))
    scratch = [
        V((2, 2, 24, HALF), F32), V((2, 2, 24, HALF), BF), V((256, 384), BF), V((256, 384), BF), V((2, 256), jnp.int32), V((2, 256), F32),
        V((2, 384, HALF), BF), V((4, 4, ROWS, CH), BF), V((4, 4, ROWS, CH), BF),
        V((4, ROWS, CH), F32), V((4, ROWS, CH), BF), V((4, ROWS, CH), BF),
        V((4, 2, 24, CH), F32), V((4, 2, 24, CH), BF), V((2, 2, 24, CH), F32), V((2, 2, 24, CH), BF), V((2, 2, 384, CH), BF),
        V((2, 2, 384, HALF), BF), V((8, 2, SLOTB, 384), BF), V((8, 2, SLOTB, 384), BF),
        V((SLOTB, 256), BF), V((8, 2, SLOTB, HALF), F32),
        V((8, 2, SLOTB, HALF), BF), V((8, 2, SLOTB, HALF), BF), V((8, 2, SLOTB, HALF), BF), V((8, 2, SLOTB, HALF), BF),
        V((8, 2, SLOTB, CH), F32),
        V((8, 2, SLOTB, CH), BF), V((8, 2, SLOTB, CH), BF), V((8, 2, SLOTB, CH), BF), V((8, 2, SLOTB, CH), BF),
        V((8, SLOTB, 384), F32), V((8, SLOTB, 384), BF), V((8, SLOTB, 384), BF),
        V((8, SLOTB, 384), BF), V((4, SLOTB, 384), BF), V((3, SLOTB, 384), BF),
        S(9), S(32), S(32), S(4), S(4), S(1), S(1), S(6), S(6), S(4), S(4), S(32), S(32), S(2), S(2), S(16), S(16), S(16), S(16),
        S(32), S(32), S(32), S(32), S(8), S(8), S(7), S(7),
    ]
    new_gate, new_momentum, token_grad = pl.pallas_call(
        kernel,
        out_shape=(
            jax.ShapeDtypeStruct((24, 1024), BF),
            jax.ShapeDtypeStruct((24, 1024), F32),
            jax.ShapeDtypeStruct((256, 384), BF),
        ),
        in_specs=[hbm, hbm, hbm, smem, hbm, hbm, hbm, hbm, hbm],
        out_specs=(vmem, vmem, vmem),
        scratch_shapes=scratch,
        compiler_params=pltpu.CompilerParams(
            collective_id=0, has_side_effects=True, vmem_limit_bytes=67_000_000),
        name="diloco_swiglu",
    )(pseudo_grad[0], momentum, outer_gate, decay_index, inner_weights, tokens[0], cotangent[0], routes[0].T, route_weight[0].T)
    return new_gate, new_momentum, token_grad[None]


def solution(mesh):
    return jax.shard_map(
        local,
        mesh=mesh,
        in_specs=(
            P(("fsdp", "island"), "expert"),
            P(("fsdp", "island"), "expert"),
            P("island", "fsdp", "expert"),
            P(),
            P(None, "fsdp", "expert"),
            P("island", "expert", "fsdp"),
            P("island", "expert", "fsdp"),
            P("island", "expert", None),
            P("island", "expert", None),
        ),
        out_specs=(
            P(("fsdp", "island"), "expert"),
            P(("fsdp", "island"), "expert"),
            P("island", "expert", "fsdp"),
        ),
        check_vma=False,
    )
```

```python
import functools
import math

import jax
import jax.numpy as jnp
from jax import lax
from jax.experimental import pallas as pl
from jax.experimental.pallas import tpu as pltpu
from jax.sharding import PartitionSpec as P

MESH = pl.DeviceIdType.MESH
BF = jnp.bfloat16
F32 = jnp.float32

D = 3072
FFW = 8192
EXPERTS = 8
SCHED = 64
NX, NYL, NZ = 8, 4, 8
ISL = 16
HALF = 512
UVLAG = 2
GLAG = 2
CH = 256
SLOTB = 64
ROWS = 48
FWD = (4, 3)
BWD = (3, 4)

beta_outer = 0.9
rate_outer = 0.7
shrink_rate = 0.2


def kernel(pg, mom_h, og_h, dec, inner, tok_h, cot_h, routes_h, rw_h, o_gate, o_mom, o_tok, *scratch):
    (momb, ogb, tok, cot, routes, rw, pv, aR, aL, sf, tw_out, tw_in, mall, gall, mfin, gfin, gbuf, wbuf, xt, xc, placing, uvp, uvsR, uvsL, uvrR, uvrL, gp, gsR, gsL,
     grR, grL, sgo, sgs, sgr, zs, zrR, zrL, lsem, a_s, a_r, tw_s, tw_r, pp_s, pp_r, me_s, me_r, of_s, of_r, x_s, x_r, w_s, w_r, b_s, b_r,
     bs_s, bs_r, uv_s, uv_r, g_s, g_r, sb_s, sb_r, z_s, z_r) = scratch
    i = lax.axis_index("island")
    f = lax.axis_index("fsdp")
    z = lax.axis_index("expert")
    x, yh = i // 2, i % 2
    yl, c = f // 2, f % 2
    oc = 1 - c

    def dev(dx=0, twin=False, dyl=0, sib=False, dz=0):
        xx = (x + dx + NX) % NX if dx else x
        yy = 1 - yh if twin else yh
        ll = jnp.clip(yl + dyl, 0, NYL - 1) if dyl else yl
        cc = oc if sib else c
        zz = (z + dz + NZ) % NZ if dz else z
        return (xx * 2 + yy, ll * 2 + cc, zz)

    SIB = dev(sib=True)
    TWIN = dev(twin=True)
    TWSIB = dev(twin=True, sib=True)
    XR, XL, ZR, ZL = dev(dx=1), dev(dx=-1), dev(dz=1), dev(dz=-1)
    XRS, XLS = dev(dx=1, sib=True), dev(dx=-1, sib=True)
    YR, YL = dev(dyl=1), dev(dyl=-1)

    def rc(src, dst, ss, rs, device):
        return pltpu.make_async_remote_copy(
            src_ref=src, dst_ref=dst, send_sem=ss, recv_sem=rs, device_id=device, device_id_type=MESH)

    sends = []

    def go(src, dst, ss, rs, device):
        cp = rc(src, dst, ss, rs, device)
        cp.start()
        sends.append(cp)

    def got(dst, ss, rs, device):
        rc(dst, dst, ss, rs, device).wait_recv()

    def half_cols(half, first=0, size=HALF):
        return pl.ds(pl.multiple_of(half * HALF + first, CH), size)

    loads = [pltpu.make_async_copy(pg.at[:, half_cols(c)], pv.at[c], lsem.at[0])]
    for m in range(2):
        loads.append(pltpu.make_async_copy(
            inner.at[m, :, pl.ds(pl.multiple_of(c * HALF, HALF), HALF)], wbuf.at[m, c], lsem.at[1 + m]))
    small = [pltpu.make_async_copy(a, b, lsem.at[3 + n]) for n, (a, b) in enumerate(
        ((routes_h, routes), (rw_h, rw), (tok_h, tok), (cot_h, cot), (mom_h.at[:, half_cols(c)], momb.at[c, yh]), (og_h.at[:, half_cols(c)], ogb.at[c, yh])))]
    for cp in small[:4] + loads + small[4:]:
        cp.start()

    barrier = pltpu.get_barrier_semaphore()
    for device in (XR, XL, XRS, XLS, ZR, ZL, SIB, TWIN, TWSIB):
        pl.semaphore_signal(barrier, inc=1, device_id=device, device_id_type=MESH)

    @pl.when(yl < NYL - 1)
    def _():
        pl.semaphore_signal(barrier, inc=1, device_id=YR, device_id_type=MESH)

    @pl.when(yl > 0)
    def _():
        pl.semaphore_signal(barrier, inc=1, device_id=YL, device_id_type=MESH)

    pl.semaphore_wait(barrier, 9 + jnp.minimum(yl, 1) + jnp.minimum(NYL - 1 - yl, 1))

    def prow(j):
        return pl.ds(pl.multiple_of(j * ROWS, 16), ROWS)

    def a_step(s):
        for e in range(2):
            for ff in range(2):
                for right in (True, False):
                    hops = FWD[e] if right else BWD[e]
                    if s >= hops:
                        continue
                    buf, d0 = (aR, 0) if right else (aL, 4)
                    j = (x + hops - s) % NX if right else (x - hops + s + NX) % NX
                    if s == 0:
                        half = oc if ff else c
                        to = (XRS if right else XLS) if ff else (XR if right else XL)
                        go(pg.at[prow(j), half_cols(half, e * CH, CH)], buf.at[2 * c + e, 0],
                           a_s.at[(2 * half + e) * 8 + d0], a_r.at[(2 * c + e) * 8 + d0], to)
                    else:
                        q = 2 * ff + e
                        n = q * 8 + d0 + s
                        got(buf.at[q, s - 1], a_s.at[n - 1], a_r.at[n - 1], XR)
                        total = buf[q, s - 1].astype(F32) + pv[ff, prow(j), e * CH:(e + 1) * CH].astype(F32)
                        buf[q, s - 1] = total.astype(BF)
                        go(buf.at[q, s - 1], buf.at[q, s], a_s.at[n], a_r.at[n], XR if right else XL)

    a_step(0)
    go(pg.at[:, half_cols(oc)], pv.at[c], pp_s.at[0], pp_r.at[0], SIB)

    for m in range(2):
        go(inner.at[m, :, pl.ds(pl.multiple_of(oc * HALF, HALF), HALF)], wbuf.at[m, c], w_s.at[m], w_r.at[m], SIB)

    for n, (half, to) in enumerate(((c, TWIN), (oc, SIB), (oc, TWSIB))):
        go(mom_h.at[:, half_cols(half)], momb.at[c, yh], me_s.at[2 * n], me_r.at[2 * n], to)
        go(og_h.at[:, half_cols(half)], ogb.at[c, yh], me_s.at[2 * n + 1], me_r.at[2 * n + 1], to)

    for cp in small[:4]:
        cp.wait()
    chosen = routes[...] == 0
    hit = jnp.max(jnp.where(chosen, 1.0, 0.0), axis=0, keepdims=True)
    weight = jnp.sum(jnp.where(chosen, rw[...], 0.0), axis=0, keepdims=True)
    n_tok = hit.shape[1]
    before = (lax.broadcasted_iota(jnp.int32, (n_tok, n_tok), 0)
              < lax.broadcasted_iota(jnp.int32, (n_tok, n_tok), 1))
    rank = jnp.dot(jnp.broadcast_to(hit, (16, n_tok)).astype(BF), jnp.where(before, 1.0, 0.0).astype(BF),
                   preferred_element_type=F32)[0:1, :]
    slot_id = lax.broadcasted_iota(jnp.int32, (SLOTB, n_tok), 0).astype(F32)
    match = jnp.where((slot_id == rank) & (hit > 0.5), 1.0, 0.0)
    slot_weight = jnp.sum(match * weight, axis=1, keepdims=True)
    placing[...] = match.astype(BF)
    xt[z, c] = jnp.dot(placing[...], tok[...], preferred_element_type=F32).astype(BF)
    xc[z, c] = (jnp.dot(placing[...], cot[...], preferred_element_type=F32) * slot_weight).astype(BF)

    XB = (xt, xc)

    def b_sib(m, n, b):
        go(XB[m].at[b, c], XB[m].at[b, c], bs_s.at[m * 8 + n], bs_r.at[m * 8 + n], SIB)

    def b_step(s):
        for m in range(2):
            for right in (True, False):
                hops = FWD[m] if right else BWD[m]
                q = m * 8 + (0 if right else 4)
                if 0 < s <= hops:
                    b = (z - s + NZ) % NZ if right else (z + s) % NZ
                    got(XB[m].at[b, c], b_s.at[q + s - 1], b_r.at[q + s - 1], ZR)
                    b_out = b
                if s < hops:
                    b_out = z if s == 0 else b
                    go(XB[m].at[b_out, c], XB[m].at[b_out, c], b_s.at[q + s], b_r.at[q + s], ZR if right else ZL)
                if 0 < s <= hops:
                    b_sib(m, s if right else FWD[m] + s, b)
            if s == 0:
                b_sib(m, 0, z)

    b_step(0)

    def uv_block(k):
        d = (k + 1) // 2
        return (z - d + NZ) % NZ if (k % 2 == 1) else (z + d) % NZ

    def uv_compute(k):
        b = uv_block(k)
        d = (k + 1) // 2
        for m in range(2):
            if k == 0:
                n = 0
            elif d == 4:
                n = 4 if m == 0 else FWD[1] + 4
            else:
                n = d if k % 2 == 1 else FWD[m] + d
            got(XB[m].at[b, oc], bs_s.at[m * 8 + n], bs_r.at[m * 8 + n], SIB)
        if k == 0:
            for cp in loads[1:]:
                cp.wait()
            for m in range(2):
                got(wbuf.at[m, oc], w_s.at[m], w_r.at[m], SIB)
        for m in range(2):
            uvp[k, m] = (jnp.dot(XB[m][b, 0], wbuf[m, 0], preferred_element_type=F32)
                         + jnp.dot(XB[m][b, 1], wbuf[m, 1], preferred_element_type=F32))

    last = NYL - 1

    def inside(k):
        return (k >= 0) & (k < 8)

    def chain(k, part, sR, rR, sL, rL, ss, rs, right):
        got_all, out, base, hasin, hasout, to = (
            (rR, sR, 0, yl > 0, yl < last, YR) if right else (rL, sL, 16, yl < last, yl > 0, YL))
        for e in range(2):
            sem = base + 2 * k + e

            @pl.when(inside(k) & hasin)
            def _():
                got(got_all.at[k, e], ss.at[sem], rs.at[sem], to)

            @pl.when(inside(k) & hasout)
            def _():
                out[k, e] = (part[k, e] + got_all[k, e].astype(F32)).astype(BF)
                rc(out.at[k, e], got_all.at[k, e], ss.at[sem], rs.at[sem], to).start()

    def uv_chain(t):
        chain(t - yl * UVLAG, uvp, uvsR, uvrR, uvsL, uvrL, uv_s, uv_r, True)
        chain(t - (last - yl) * UVLAG, uvp, uvsR, uvrR, uvsL, uvrL, uv_s, uv_r, False)

    @pl.when(yl == 0)
    def _():
        uvrR[...] = jnp.zeros_like(uvrR)
        grR[...] = jnp.zeros_like(grR)

    @pl.when(yl == last)
    def _():
        uvrL[...] = jnp.zeros_like(uvrL)
        grL[...] = jnp.zeros_like(grL)

    loads[0].wait()
    got(pv.at[oc], pp_s.at[0], pp_r.at[0], SIB)
    a_step(1)
    b_step(1)
    uv_compute(0)
    uv_chain(0)
    a_step(2)
    uv_compute(1)
    b_step(2)
    uv_chain(1)
    a_step(3)
    uv_compute(2)
    b_step(3)
    uv_compute(3)
    uv_chain(2)

    for e in range(2):
        for ff in range(2):
            q = 2 * ff + e
            total = pv[ff, prow(x), e * CH:(e + 1) * CH].astype(F32)
            for buf, hops, n in ((aR, FWD[e], q * 8), (aL, BWD[e], q * 8 + 4)):
                got(buf.at[q, hops - 1], a_s.at[n + hops - 1], a_r.at[n + hops - 1], XR)
                total = total + buf[q, hops - 1].astype(F32)
            sf[q] = total
            tw_out[q] = total.astype(BF)
            go(tw_out.at[q], tw_in.at[q], tw_s.at[q], tw_r.at[q], TWIN)
    uv_compute(4)
    uv_compute(5)
    b_step(4)
    uv_chain(3)
    uv_compute(6)
    uv_compute(7)

    step_value = jnp.full((8, 128), dec[0], jnp.int32).astype(F32)
    rate = (rate_outer * 0.5 * (1.0 + jnp.cos(math.pi * step_value / SCHED)))[0:1, 0:1]
    for cp in small[4:]:
        cp.wait()
    for n, (ff, hh, to) in enumerate(((c, 1 - yh, TWIN), (oc, yh, SIB), (oc, 1 - yh, TWSIB))):
        got(momb.at[ff, hh], me_s.at[2 * n], me_r.at[2 * n], to)
        got(ogb.at[ff, hh], me_s.at[2 * n + 1], me_r.at[2 * n + 1], to)

    def outer_step(e):
        where = slice(e * CH, (e + 1) * CH)
        for ff in range(2):
            q = 2 * ff + e
            got(tw_in.at[q], tw_s.at[q], tw_r.at[q], TWIN)
            mean_grad = (sf[q] + tw_in[q].astype(F32)) * (1.0 / ISL)
            old = jnp.concatenate([momb[ff, 0, :, where], momb[ff, 1, :, where]], axis=0)
            outer = jnp.concatenate([ogb[ff, 0, :, where].astype(F32), ogb[ff, 1, :, where].astype(F32)], axis=0)
            momentum_new = beta_outer * old + mean_grad
            gate_new = (1.0 - shrink_rate * rate) * outer - rate * (mean_grad + beta_outer * momentum_new)
            gbuf[e, ff, prow(x), :] = gate_new.astype(BF)
            for hh in range(2):
                mall[q, hh] = momentum_new[hh * 24:(hh + 1) * 24]
                gall[q, hh] = gate_new[hh * 24:(hh + 1) * 24].astype(BF)

    def hand_out(e):
        mfin[c, e] = mall[2 * c + e, yh]
        gfin[c, e] = gall[2 * c + e, yh]
        go(mall.at[2 * oc + e, yh], mfin.at[c, e], of_s.at[2 * e], of_r.at[2 * e], SIB)
        go(gall.at[2 * oc + e, yh], gfin.at[c, e], of_s.at[2 * e + 1], of_r.at[2 * e + 1], SIB)

    def x_step(s, e):
        for h in range(2):
            for right in (True, False):
                hops = FWD[h] if right else BWD[h]
                n = (e * 2 + h) * 8 + (0 if right else 4)
                j = (x - s + NX) % NX if right else (x + s) % NX
                here = gbuf.at[e, h, prow(j), :]
                if 0 < s <= hops:
                    got(here, x_s.at[n + s - 1], x_r.at[n + s - 1], XR)
                if s < hops:
                    go(here, here, x_s.at[n + s], x_r.at[n + s], XR if right else XL)

    for e in range(2):
        outer_step(e)
        x_step(0, e)
    uv_chain(4)
    for e in range(2):
        hand_out(e)
    uv_chain(5)
    for s in range(1, 4):
        for e in range(2):
            x_step(s, e)
        uv_chain(5 + s)

    in_scale = D ** (-0.5)
    out_scale = FFW ** (-0.5)

    def block_of(k):
        m = 4 - (k + 1) // 2
        sign = 1 - 2 * ((k + 1) % 2)
        return (z + m * sign + NZ) % NZ

    def swiglu(pre, uv):
        pre_gate = in_scale * pre
        pre_up = in_scale * uv[0]
        back = out_scale * uv[1]
        s = jax.nn.sigmoid(pre_gate)
        gu = back * pre_gate * s
        gg = back * pre_up * s * (1.0 + pre_gate * (1.0 - s))
        return gg.astype(BF), gu.astype(BF)

    def g_compute(k, parts=(0, 1)):
        b = block_of(k)
        for e in parts:
            gp[k, e] = (jnp.dot(xt[b, 0], gbuf[e, 0], preferred_element_type=F32)
                        + jnp.dot(xt[b, 1], gbuf[e, 1], preferred_element_type=F32))

    def back(k):
        u = 7 - k
        dims = (((1,), (1,)), ((), ()))
        grads = []
        for e in range(2):
            where = slice(e * CH, (e + 1) * CH)
            pre = gp[k, e] + grR[k, e].astype(F32) + grL[k, e].astype(F32)
            uv = [uvp[u, m, :, where] + uvrR[u, m, :, where].astype(F32) + uvrL[u, m, :, where].astype(F32) for m in range(2)]
            grads.append(swiglu(pre, uv))

        def part(ff):
            total = 0.0
            for e, (gg, gu) in enumerate(grads):
                total = total + lax.dot_general(gg, gbuf[e, ff], dims, preferred_element_type=F32)
                total = total + lax.dot_general(
                    gu, wbuf[0, ff, :, e * CH:(e + 1) * CH], dims, preferred_element_type=F32)
            return in_scale * total

        sgs[k] = part(oc).astype(BF)
        rc(sgs.at[k], sgr.at[k], sb_s.at[k], sb_r.at[k], SIB).start()
        sgo[k] = part(c)

    def z_stage(k):
        got(sgr.at[k], sb_s.at[k], sb_r.at[k], SIB)
        own = sgo[k] + sgr[k].astype(F32)

        @pl.when(k == 0)
        def _():
            zs[k] = own.astype(BF)
            rc(zs.at[k], zrR.at[0], z_s.at[0], z_r.at[0], ZR).start()

        @pl.when((k % 2 == 1) & (k < 7))
        def _():
            s = (k + 1) // 2
            got(zrR.at[s - 1], z_s.at[s - 1], z_r.at[s - 1], ZR)
            zs[k] = (own + zrR[s - 1].astype(F32)).astype(BF)
            rc(zs.at[k], zrR.at[s], z_s.at[s], z_r.at[s], ZR).start()

        @pl.when(k == 2)
        def _():
            zs[k] = own.astype(BF)
            rc(zs.at[k], zrL.at[0], z_s.at[4], z_r.at[4], ZL).start()

        @pl.when((k % 2 == 0) & (k > 2))
        def _():
            s = k // 2 - 1
            got(zrL.at[s - 1], z_s.at[4 + s - 1], z_r.at[4 + s - 1], ZL)
            zs[k] = (own + zrL[s - 1].astype(F32)).astype(BF)
            rc(zs.at[k], zrL.at[s], z_s.at[4 + s], z_r.at[4 + s], ZL).start()

        @pl.when(k == 7)
        def _():
            got(zrR.at[3], z_s.at[3], z_r.at[3], ZR)
            got(zrL.at[2], z_s.at[6], z_r.at[6], ZL)
            slot_grads = (own + zrR[3].astype(F32) + zrL[2].astype(F32)).astype(BF)
            o_tok[...] = lax.dot_general(
                placing[...], slot_grads, (((0,), (0,)), ((), ())), preferred_element_type=F32).astype(BF)

    def finish_early():
        for e in range(2):
            got(mfin.at[oc, e], of_s.at[2 * e], of_r.at[2 * e], SIB)
            got(gfin.at[oc, e], of_s.at[2 * e + 1], of_r.at[2 * e + 1], SIB)
            for half in range(2):
                where = slice(half * HALF + e * CH, half * HALF + (e + 1) * CH)
                o_mom[:, where] = mfin[half, e]
                o_gate[:, where] = gfin[half, e]

        for cp in sends:
            cp.wait_send()

    def tick(t, carry):
        def stage(k, fn):
            @pl.when(inside(k))
            def _():
                fn(k)

        @pl.when(t == 4)
        def _():
            finish_early()

        chain(t - yl * GLAG, gp, gsR, grR, gsL, grL, g_s, g_r, True)
        chain(t - (last - yl) * GLAG, gp, gsR, grR, gsL, grL, g_s, g_r, False)
        uv_chain(t + 9)
        stage(t - last * GLAG, back)
        stage(t - last * GLAG - 1, z_stage)
        stage(t + 1, g_compute)
        return carry

    for e in range(2):
        x_step(4, e)
        g_compute(0, (e,))
    lax.fori_loop(0, 8 + last * GLAG + 1, tick, None)

    def drain(k, carry):
        for e in range(2):
            n = 2 * k + e

            @pl.when(yl < last)
            def _():
                rc(uvsR.at[k, e], uvrR.at[k, e], uv_s.at[n], uv_r.at[n], YR).wait_send()
                rc(gsR.at[k, e], grR.at[k, e], g_s.at[n], g_r.at[n], YR).wait_send()

            @pl.when(yl > 0)
            def _():
                rc(uvsL.at[k, e], uvrL.at[k, e], uv_s.at[16 + n], uv_r.at[16 + n], YL).wait_send()
                rc(gsL.at[k, e], grL.at[k, e], g_s.at[16 + n], g_r.at[16 + n], YL).wait_send()

        rc(sgs.at[k], sgr.at[k], sb_s.at[k], sb_r.at[k], SIB).wait_send()

        @pl.when(k < 7)
        def _():
            rc(zs.at[k], zs.at[k], z_s.at[k], z_r.at[k], ZR).wait_send()

        return carry

    lax.fori_loop(0, 8, drain, None)


def write_out(a, b, c, oa, ob, oc, sem):
    copies = [pltpu.make_async_copy(src, dst, sem.at[n]) for n, (src, dst) in enumerate(((a, oa), (b, ob), (c, oc)))]
    for cp in copies:
        cp.start()
    for cp in copies:
        cp.wait()


def local(outer_gate, momentum, pseudo_grad, decay_index, inner_weights, tokens, cotangent, routes, route_weight):
    vmem = pl.BlockSpec(memory_space=pltpu.VMEM)
    hbm = pl.BlockSpec(memory_space=pltpu.HBM)
    smem = pl.BlockSpec(memory_space=pltpu.SMEM)
    V = pltpu.VMEM
    S = lambda n: pltpu.SemaphoreType.DMA((n,))
    scratch = [
        V((2, 2, 24, HALF), F32), V((2, 2, 24, HALF), BF), V((256, 384), BF), V((256, 384), BF), V((2, 256), jnp.int32), V((2, 256), F32),
        V((2, 384, HALF), BF), V((4, 4, ROWS, CH), BF), V((4, 4, ROWS, CH), BF),
        V((4, ROWS, CH), F32), V((4, ROWS, CH), BF), V((4, ROWS, CH), BF),
        V((4, 2, 24, CH), F32), V((4, 2, 24, CH), BF), V((2, 2, 24, CH), F32), V((2, 2, 24, CH), BF), V((2, 2, 384, CH), BF),
        V((2, 2, 384, HALF), BF), V((8, 2, SLOTB, 384), BF), V((8, 2, SLOTB, 384), BF),
        V((SLOTB, 256), BF), V((8, 2, SLOTB, HALF), F32),
        V((8, 2, SLOTB, HALF), BF), V((8, 2, SLOTB, HALF), BF), V((8, 2, SLOTB, HALF), BF), V((8, 2, SLOTB, HALF), BF),
        V((8, 2, SLOTB, CH), F32),
        V((8, 2, SLOTB, CH), BF), V((8, 2, SLOTB, CH), BF), V((8, 2, SLOTB, CH), BF), V((8, 2, SLOTB, CH), BF),
        V((8, SLOTB, 384), F32), V((8, SLOTB, 384), BF), V((8, SLOTB, 384), BF),
        V((8, SLOTB, 384), BF), V((4, SLOTB, 384), BF), V((3, SLOTB, 384), BF),
        S(9), S(32), S(32), S(4), S(4), S(1), S(1), S(6), S(6), S(4), S(4), S(32), S(32), S(2), S(2), S(16), S(16), S(16), S(16),
        S(32), S(32), S(32), S(32), S(8), S(8), S(7), S(7),
    ]
    new_gate, new_momentum, token_grad = pl.pallas_call(
        kernel,
        out_shape=(
            jax.ShapeDtypeStruct((24, 1024), BF),
            jax.ShapeDtypeStruct((24, 1024), F32),
            jax.ShapeDtypeStruct((256, 384), BF),
        ),
        in_specs=[hbm, hbm, hbm, smem, hbm, hbm, hbm, hbm, hbm],
        out_specs=(vmem, vmem, vmem),
        scratch_shapes=scratch,
        compiler_params=pltpu.CompilerParams(
            collective_id=0, has_side_effects=True, vmem_limit_bytes=67_000_000),
        name="diloco_swiglu",
    )(pseudo_grad[0], momentum, outer_gate, decay_index, inner_weights, tokens[0], cotangent[0], routes[0].T, route_weight[0].T)
    new_gate, new_momentum, token_grad = pl.pallas_call(
        write_out,
        out_shape=tuple(jax.ShapeDtypeStruct(a.shape, a.dtype) for a in (new_gate, new_momentum, token_grad)),
        in_specs=[vmem, vmem, vmem],
        out_specs=(hbm, hbm, hbm),
        scratch_shapes=[S(3)],
        name="write_out",
    )(new_gate, new_momentum, token_grad)
    return new_gate, new_momentum, token_grad[None]


def solution(mesh):
    return jax.shard_map(
        local,
        mesh=mesh,
        in_specs=(
            P(("fsdp", "island"), "expert"),
            P(("fsdp", "island"), "expert"),
            P("island", "fsdp", "expert"),
            P(),
            P(None, "fsdp", "expert"),
            P("island", "expert", "fsdp"),
            P("island", "expert", "fsdp"),
            P("island", "expert", None),
            P("island", "expert", None),
        ),
        out_specs=(
            P(("fsdp", "island"), "expert"),
            P(("fsdp", "island"), "expert"),
            P("island", "expert", "fsdp"),
        ),
        check_vma=False,
    )
```
